32 devices in a mesh: grp: 2 (over x), seq: 8 (over z, y), head: 2 (over core).
Axes of the slice: x: 2, y: 2, z: 4, core: 2. Of those that a mesh axis runs over, the one named last changes fastest.
Arguments:
- queries: bfloat16 [16384, 2048], P(('grp', 'seq'), 'head'), parts along dimension 0, may hold values from -6 to 6
- key_states: bfloat16 [16384, 1024], P(('grp', 'seq'), 'head'), parts along dimension 0, may hold values from -6 to 6
- value_states: bfloat16 [16384, 1024], P(('grp', 'seq'), 'head'), parts along dimension 0, may hold values from -6 to 6
- segment_ids: int32 [16384], P(('grp', 'seq')), parts along dimension 0, may hold values from 0 to 15, as said below
Outputs:
- attended: bfloat16 [16384, 2048], P(('grp', 'seq'), 'head'), parts along dimension 0
The draws below stay inside these ranges and needn't reach their ends.
There are 2 independent parts, one for each index of `grp`. The reference program is written for one: setup_inputs(seed, part) draws one part's arguments, and reference() takes and returns one part's arrays. A program takes and returns all parts, laid end to end along the dimension named above; each array names one. Nothing has to cross between parts.
Inputs may be any that keep to these rules, and one draw needn't show every extreme that they name: `segment_ids`: read in logical order, the ids never fall, start at 0 and name all 16 candidates, each one token or more; the first 1536 and the last 1536 logical tokens each lie within one candidate.
All inputs are finite; a program needn't handle non-finite values.
Results may differ from the reference program's by a relative error of at most 0.008.
Values may be sent and summed in bfloat16 or wider, within the bound.
No kernel may reach another device: no remote copies, remote signals or barrier semaphores. Data moves between devices by JAX's collectives and lax.ppermute only.
A program may use at most 64 MiB of HBM per device.

```python
import jax
import jax.numpy as jnp
from jax import lax

HEAD_DIM = 128
QHEADS = 16
KVHEADS = 8
WINDOW = 1024
TOK_DEV = 1024
TOKENS = 8192
CANDS = 16
N_SEQ = 8


def draw_queries(key, part):
    shape_all = (TOKENS, QHEADS * HEAD_DIM)
    return jax.random.truncated_normal(jax.random.fold_in(key, 1), -6.0, 6.0, shape_all, jnp.float32).astype(jnp.bfloat16)


def draw_key_states(key, part):
    shape_all = (TOKENS, KVHEADS * HEAD_DIM)
    return jax.random.truncated_normal(jax.random.fold_in(key, 2), -6.0, 6.0, shape_all, jnp.float32).astype(jnp.bfloat16)


def draw_segment_ids(key, part):
    span_rows = TOK_DEV // 2
    seq_count = TOKENS // TOK_DEV
    room = TOKENS - 6 * span_rows + 1
    starts = jax.random.permutation(jax.random.fold_in(key, 3), room)[:CANDS - 1] + 3 * span_rows
    flags = jnp.zeros((TOKENS,), jnp.int32).at[starts].set(1)
    logical = jnp.cumsum(flags).astype(jnp.int32)
    blocks = logical.reshape(2 * seq_count, span_rows)
    return jnp.stack([blocks[:seq_count], blocks[seq_count:][::-1]], axis=1).reshape(TOKENS)


def level_of(rng, shape, pieces, least, largest):
    factor_of, own = 1.0, jax.random.fold_in(rng, 6)
    for dim, parts in pieces:
        draws = jnp.exp(jax.random.uniform(jax.random.fold_in(own, dim), (parts,), jnp.float32, least / len(pieces), largest / len(pieces)))
        factor_of = factor_of * jnp.repeat(draws, shape[dim] // parts).reshape([-1 if axis == dim else 1 for axis in range(len(shape))])
    return factor_of


def centred(rng, dims, scale, bound, split=(), kind=jnp.bfloat16):
    gain = level_of(rng, dims, split, -0.22, 0.18) if split else 1.0
    values = jax.random.normal(rng, dims, jnp.float32) * scale * gain
    return jnp.minimum(jnp.maximum(values, -bound), bound).astype(kind)


def setup_inputs(seed: int = 0, part: int = 0) -> dict:
    arg_keys = jax.random.split(jax.random.key(seed), 5)
    own_keys = jax.random.split(jax.random.fold_in(arg_keys[4], part), 5)
    return {
        "queries": draw_queries(jax.random.fold_in(jax.random.fold_in(arg_keys[4], part), 71), part),
        "key_states": draw_key_states(jax.random.fold_in(jax.random.fold_in(arg_keys[4], part), 71), part),
        "value_states": centred(own_keys[2], (TOKENS, KVHEADS * HEAD_DIM), 1.0, 6.0, ((0, 8), (1, 2))),
        "segment_ids": draw_segment_ids(jax.random.fold_in(jax.random.fold_in(arg_keys[4], part), 71), part),
    }


attn_scale = 168.0 ** -0.5


def reference(queries, key_states, value_states, segment_ids):
    span_rows = TOK_DEV // 2
    seq_count = N_SEQ
    groups = QHEADS // KVHEADS

    def unfold(stored):
        blocks = stored.reshape((seq_count, 2, span_rows) + stored.shape[1:])
        return jnp.concatenate([blocks[:, 0], blocks[::-1, 1]], axis=0).reshape(stored.shape)

    def refold(logical):
        blocks = logical.reshape((2 * seq_count, span_rows) + logical.shape[1:])
        return jnp.stack([blocks[:seq_count], blocks[seq_count:][::-1]], axis=1).reshape(logical.shape)

    query_log = unfold(queries)
    key_log = jnp.concatenate([jnp.zeros((2 * span_rows, key_states.shape[1]), key_states.dtype), unfold(key_states)], axis=0)
    value_log = jnp.concatenate([jnp.zeros((2 * span_rows, value_states.shape[1]), value_states.dtype), unfold(value_states)], axis=0)
    seg_log = unfold(segment_ids)
    seg_pad = jnp.concatenate([jnp.full((2 * span_rows,), -1, jnp.int32), seg_log.astype(jnp.int32)], axis=0)

    def one_span(block):
        start = (block * span_rows).astype(jnp.int32)
        query_blk = lax.dynamic_slice_in_dim(query_log, start, span_rows, 0)
        key_blk = lax.dynamic_slice_in_dim(key_log, start, 3 * span_rows, 0)
        value_blk = lax.dynamic_slice_in_dim(value_log, start, 3 * span_rows, 0)
        query_seg = lax.dynamic_slice_in_dim(seg_log, start, span_rows, 0)
        key_seg = lax.dynamic_slice_in_dim(seg_pad, start, 3 * span_rows, 0)
        query_pos = start + jnp.arange(span_rows, dtype=jnp.int32)
        key_pos = start - 2 * span_rows + jnp.arange(3 * span_rows, dtype=jnp.int32)
        visible = (key_pos[None, :] <= query_pos[:, None]) & (key_pos[None, :] > query_pos[:, None] - WINDOW)
        visible = visible & (key_pos[None, :] >= 0) & (key_seg[None, :] == query_seg[:, None])
        query_four = query_blk.astype(jnp.float32).reshape(span_rows, KVHEADS, groups, HEAD_DIM)
        key_three = key_blk.astype(jnp.float32).reshape(3 * span_rows, KVHEADS, HEAD_DIM)
        value_three = value_blk.astype(jnp.float32).reshape(3 * span_rows, KVHEADS, HEAD_DIM)
        scores = jnp.einsum("qhgd,khd->hgqk", query_four, key_three) * attn_scale
        scores = jnp.where(visible[None, None], scores, jnp.float32(-1e30))
        row_max = jnp.max(scores, axis=-1, keepdims=True)
        exp_terms = jnp.exp(scores - row_max)
        weights = (exp_terms / jnp.sum(exp_terms, axis=-1, keepdims=True)).astype(jnp.bfloat16)
        mixed_out = jnp.einsum("hgqk,khd->qhgd", weights.astype(jnp.float32), value_three)
        return mixed_out.astype(jnp.bfloat16).reshape(span_rows, QHEADS * HEAD_DIM)

    outputs = lax.map(one_span, jnp.arange(2 * seq_count, dtype=jnp.int32))
    return refold(outputs.reshape(2 * seq_count * span_rows, QHEADS * HEAD_DIM))
```

```python
import functools
import math

import jax
import jax.numpy as jnp
from jax import lax
from jax.experimental import pallas as pl
from jax.experimental.pallas import tpu as pltpu
from jax.sharding import PartitionSpec as P

HEAD_DIM = 128
GROUPS = 2
HALF = 512
PAIR = 2
TILE = 256

EXP_SCALE = 168.0 ** (-0.5) * math.log2(math.e)
HIDDEN = -1e30

VMEM = pl.BlockSpec(memory_space=pltpu.VMEM)
SMEM = pl.BlockSpec(memory_space=pltpu.SMEM)
HBM = pl.BlockSpec(memory_space=pl.ANY)
PARAMS = pltpu.CompilerParams(vmem_limit_bytes=24 << 20)


def dot_nt(a, b):
    return lax.dot_general(
        a, b, (((1,), (1,)), ((), ())), preferred_element_type=jnp.float32
    )


def dot_nn(a, b):
    return lax.dot_general(
        a, b, (((1,), (0,)), ((), ())), preferred_element_type=jnp.float32
    )


def head_cols(head):
    return slice(head * HEAD_DIM, (head + 1) * HEAD_DIM)


def lane_sum(p):
    total = p[:, :HEAD_DIM]
    for c in range(1, p.shape[1] // HEAD_DIM):
        total = total + p[:, head_cols(c)]
    return total


def same_segment(query_seg, key_seg):
    chunks = key_seg.shape[1] // HEAD_DIM
    return jnp.concatenate([query_seg] * chunks, axis=1) == key_seg


def pack_kernel(k, v, srow, f1, f2, fz, b1, b2, bz):
    for role, (one, two, both) in enumerate(((f1, f2, fz), (b1, b2, bz))):
        rows = slice(role * HALF, (role + 1) * HALF)
        for h, piece in enumerate((one, two)):
            cols = slice(h * 2 * HEAD_DIM, (h + 1) * 2 * HEAD_DIM)
            for part, src in enumerate((k, v)):
                to = slice(part * 2 * HEAD_DIM, (part + 1) * 2 * HEAD_DIM)
                data = src[rows, cols]
                piece[0:HALF, to] = data
                both[h * HALF : (h + 1) * HALF, to] = data
        ids = srow[:, rows].astype(jnp.bfloat16)
        one[HALF : HALF + 8, :] = ids
        both[2 * HALF : 2 * HALF + 8, :] = ids


def pack(k, v, srow):
    def shape(rows):
        return jax.ShapeDtypeStruct((rows, HALF), jnp.bfloat16)

    one = (shape(HALF + 8), shape(HALF), shape(2 * HALF + 8))
    return pl.pallas_call(
        pack_kernel,
        out_shape=one + one,
        in_specs=[VMEM] * 3,
        out_specs=[VMEM] * 6,
        compiler_params=PARAMS,
        cost_estimate=pl.CostEstimate(
            flops=1 << 20, bytes_accessed=6 << 20, transcendentals=0
        ),
        name="pack",
    )(k, v, srow)


def stacked_queries(q, rows, first_head):
    return jnp.concatenate(
        [q[rows, head_cols(first_head + j)] for j in range(GROUPS)], axis=0
    )


def near_kernel(h, n, idx, q, k, v, sq, srow, zp, zm, pa, pb, acc, mx, ls):
    from_partner = idx[0] >= n - 2
    piece = (pa, pb)[h]
    for role in range(2):
        base = role * HALF
        seg_far = zp[2 * HALF : 2 * HALF + 1, :]
        if role == 1:
            seg_far = jnp.where(
                from_partner, pa[HALF : HALF + 1, :], zm[2 * HALF : 2 * HALF + 1, :]
            )
        seg_far = seg_far.astype(jnp.float32)
        for g in range(PAIR):
            kcol = head_cols(g)
            vcol = head_cols(PAIR + g)
            own = head_cols(PAIR * h + g)
            far_rows = slice(h * HALF, (h + 1) * HALF)
            if role == 0:
                k_far = zp[far_rows, kcol]
                v_far = zp[far_rows, vcol]
            else:
                k_far = jnp.where(from_partner, piece[0:HALF, kcol], zm[far_rows, kcol])
                v_far = jnp.where(from_partner, piece[0:HALF, vcol], zm[far_rows, vcol])
            for i in range(HALF // TILE):
                rows = slice(base + i * TILE, base + (i + 1) * TILE)
                q2 = stacked_queries(q, rows, (PAIR * h + g) * GROUPS)
                n_own = (i + 1) * TILE
                s_own = dot_nt(q2, k[base : base + n_own, own])
                s_far = dot_nt(q2, k_far[i * TILE :])
                seg_q = sq[rows, :]
                see_own = same_segment(seg_q, srow[0:1, base : base + n_own])
                see_far = same_segment(seg_q, seg_far[:, i * TILE :])
                r = lax.broadcasted_iota(jnp.int32, see_own.shape, 0) + i * TILE
                c = lax.broadcasted_iota(jnp.int32, see_own.shape, 1)
                see_own = see_own & (c <= r)
                r = lax.broadcasted_iota(jnp.int32, see_far.shape, 0)
                c = lax.broadcasted_iota(jnp.int32, see_far.shape, 1)
                see_far = see_far & (c > r)
                s_own = jnp.where(jnp.concatenate([see_own] * GROUPS, axis=0), s_own, HIDDEN)
                s_far = jnp.where(jnp.concatenate([see_far] * GROUPS, axis=0), s_far, HIDDEN)
                m = jnp.maximum(
                    jnp.max(s_own, axis=-1, keepdims=True),
                    jnp.max(s_far, axis=-1, keepdims=True),
                )
                p_own = jnp.exp2((s_own - m) * EXP_SCALE)
                p_far = jnp.exp2((s_far - m) * EXP_SCALE)
                part = lane_sum(p_own) + lane_sum(p_far)
                o = dot_nn(p_own.astype(jnp.bfloat16), v[base : base + n_own, own])
                o = o + dot_nn(p_far.astype(jnp.bfloat16), v_far[i * TILE :])
                m = jnp.broadcast_to(m, part.shape)
                for j in range(GROUPS):
                    col = head_cols(GROUPS * g + j)
                    mine = slice(j * TILE, (j + 1) * TILE)
                    acc[rows, col] = o[mine]
                    mx[rows, col] = m[mine]
                    ls[rows, col] = part[mine]


def near(h, n, idx, q, k, v, sq, srow, zp, zm, pa, pb):
    state = jax.ShapeDtypeStruct((2 * HALF, 2 * PAIR * HEAD_DIM), jnp.float32)
    return pl.pallas_call(
        functools.partial(near_kernel, h, n),
        out_shape=(state,) * 3,
        in_specs=[SMEM] + [VMEM] * 9,
        out_specs=[VMEM] * 3,
        compiler_params=PARAMS,
        cost_estimate=pl.CostEstimate(
            flops=3 << 30, bytes_accessed=12 << 20, transcendentals=3 << 20
        ),
        name=f"near{h}",
    )(idx, q, k, v, sq, srow, zp, zm, pa, pb)


def last_kernel(h, role, n, idx, q, sq, alt_a, alt_b, alt_seg, kv, kv_seg, acc, mx, ls, *rest):
    out, o_buf, sem = rest[-3:]
    base = role * HALF
    if role == 0:
        use_alt = idx[0] % 2 == 1
        seg = jnp.where(use_alt, alt_seg[HALF : HALF + 1, :], kv_seg[HALF : HALF + 1, :])
        seg = seg.astype(jnp.float32)
    else:
        use_alt = idx[0] == n - 1
        seg = jnp.where(
            use_alt, alt_seg[0:1, 0:HALF], kv_seg[HALF : HALF + 1, :].astype(jnp.float32)
        )
    for g in range(PAIR):
        if role == 0:
            k_alt = alt_a[0:HALF, head_cols(g)]
            v_alt = alt_a[0:HALF, head_cols(PAIR + g)]
        else:
            k_alt = alt_a[0:HALF, head_cols(PAIR * h + g)]
            v_alt = alt_b[0:HALF, head_cols(PAIR * h + g)]
        k_mid = jnp.where(use_alt, k_alt, kv[0:HALF, head_cols(g)])
        v_mid = jnp.where(use_alt, v_alt, kv[0:HALF, head_cols(PAIR + g)])
        for i in range(HALF // TILE):
            rows = slice(base + i * TILE, base + (i + 1) * TILE)
            q2 = stacked_queries(q, rows, (PAIR * h + g) * GROUPS)
            s = dot_nt(q2, k_mid)
            see = same_segment(sq[rows, :], seg)
            s = jnp.where(jnp.concatenate([see] * GROUPS, axis=0), s, HIDDEN)
            cols = [head_cols(GROUPS * g + j) for j in range(GROUPS)]
            m_old = jnp.concatenate([mx[rows, c] for c in cols], axis=0)
            l_old = jnp.concatenate([ls[rows, c] for c in cols], axis=0)
            a_old = jnp.concatenate([acc[rows, c] for c in cols], axis=0)
            m = jnp.maximum(m_old, jnp.max(s, axis=-1, keepdims=True))
            keep = jnp.exp2((m_old - m) * EXP_SCALE)
            p = jnp.exp2((s - jnp.concatenate([m] * (HALF // HEAD_DIM), axis=1)) * EXP_SCALE)
            total = jnp.sum(keep * l_old + lane_sum(p), axis=-1, keepdims=True)
            o = keep * a_old + dot_nn(p.astype(jnp.bfloat16), v_mid)
            o = (o * (1.0 / total)).astype(jnp.bfloat16)
            for j in range(GROUPS):
                o_buf[i * TILE : (i + 1) * TILE, cols[j]] = o[j * TILE : (j + 1) * TILE]
    width = 2 * PAIR * HEAD_DIM
    copy = pltpu.make_async_copy(
        o_buf, out.at[pl.ds(base, HALF), pl.ds(h * width, width)], sem
    )
    copy.start()
    copy.wait()


def last(h, role, n, idx, q, sq, alt_a, alt_b, alt_seg, kv, kv_seg, state, out):
    args = (idx, q, sq, alt_a, alt_b, alt_seg, kv, kv_seg) + state
    aliases = {}
    specs = [SMEM] + [VMEM] * (len(args) - 1)
    if out is not None:
        aliases = {len(args): 0}
        args = args + (out,)
        specs.append(HBM)
    return pl.pallas_call(
        functools.partial(last_kernel, h, role, n),
        out_shape=jax.ShapeDtypeStruct(q.shape, q.dtype),
        in_specs=specs,
        out_specs=HBM,
        input_output_aliases=aliases,
        scratch_shapes=[
            pltpu.VMEM((HALF, 2 * PAIR * HEAD_DIM), jnp.bfloat16),
            pltpu.SemaphoreType.DMA,
        ],
        compiler_params=PARAMS,
        cost_estimate=pl.CostEstimate(
            flops=1 << 30, bytes_accessed=5 << 20, transcendentals=1 << 20
        ),
        name=f"last{h}{role}",
    )(*args)


def body(queries, key_states, value_states, segment_ids):
    n = lax.axis_size("seq")
    idx = lax.axis_index("seq").astype(jnp.int32).reshape(1)
    ids = segment_ids.astype(jnp.float32) + 1.0
    srow = jnp.broadcast_to(ids[None, :], (8, 2 * HALF))
    sq = jnp.broadcast_to(ids[:, None], (2 * HALF, HEAD_DIM))

    f1, f2, fz, b1, b2, bz = pack(key_states, value_states, srow)

    partner = [(i, i ^ 1) for i in range(n)]
    up_two = [(i, i + 2) for i in range(n - 2)]
    down_two = [(i + 2, i) for i in range(n - 2)]
    down_one = [(i + 1, i) for i in range(n - 1)]
    relay = [(i, i + 2) for i in range(0, n - 2, 2)]

    def send(x, route):
        return lax.ppermute(x, "seq", route)

    pa = send(f1, partner)
    zp = send(fz, up_two)
    zm = send(bz, down_two)
    pb = send(f2, partner)
    d1 = send(b1, down_one)
    d2 = send(b2, down_one)
    r1 = send(pa, relay)
    r2 = send(pb, relay)

    state1 = near(0, n, idx, queries, key_states, value_states, sq, srow, zp, zm, pa, pb)
    state2 = near(1, n, idx, queries, key_states, value_states, sq, srow, zp, zm, pa, pb)
    out = last(0, 0, n, idx, queries, sq, pa, pa, pa, r1, r1, tuple(state1), None)
    out = last(
        0, 1, n, idx, queries, sq, key_states, value_states, srow, d1, d1, tuple(state1), out
    )
    out = last(1, 0, n, idx, queries, sq, pb, pb, pa, r2, r1, tuple(state2), out)
    out = last(
        1, 1, n, idx, queries, sq, key_states, value_states, srow, d2, d1, tuple(state2), out
    )
    return out


def solution(mesh):
    in_specs = (
        P(("grp", "seq"), "head"),
        P(("grp", "seq"), "head"),
        P(("grp", "seq"), "head"),
        P(("grp", "seq")),
    )
    out_specs = P(("grp", "seq"), "head")
    return jax.shard_map(body, mesh=mesh, in_specs=in_specs, out_specs=out_specs, check_vma=False)
```

```python
import functools
import math

import jax
import jax.numpy as jnp
from jax import lax
from jax.experimental import pallas as pl
from jax.experimental.pallas import tpu as pltpu
from jax.sharding import PartitionSpec as P

HEAD_DIM = 128
GROUPS = 2
HALF = 512
PAIR = 2
TILE = 256

EXP_SCALE = 168.0 ** (-0.5) * math.log2(math.e)
HIDDEN = -1e30

VMEM = pl.BlockSpec(memory_space=pltpu.VMEM)
SMEM = pl.BlockSpec(memory_space=pltpu.SMEM)
ANY = pl.BlockSpec(memory_space=pl.ANY)
HBM = pl.BlockSpec(memory_space=pltpu.HBM)
PARAMS = pltpu.CompilerParams(vmem_limit_bytes=24 << 20)


def dot_nt(a, b):
    return lax.dot_general(
        a, b, (((1,), (1,)), ((), ())), preferred_element_type=jnp.float32
    )


def dot_nn(a, b):
    return lax.dot_general(
        a, b, (((1,), (0,)), ((), ())), preferred_element_type=jnp.float32
    )


def head_cols(head):
    return slice(head * HEAD_DIM, (head + 1) * HEAD_DIM)


def lane_sum(p):
    total = p[:, :HEAD_DIM]
    for c in range(1, p.shape[1] // HEAD_DIM):
        total = total + p[:, head_cols(c)]
    return total


def same_segment(query_seg, key_seg):
    chunks = key_seg.shape[1] // HEAD_DIM
    return jnp.concatenate([query_seg] * chunks, axis=1) == key_seg


def pack_kernel(k, v, ids, f1, f2, fz, b1, b2, sem):
    copies = []
    for role, pieces in enumerate(((f1, f2), (b1, b2))):
        rows = pl.ds(role * HALF, HALF)
        for h, piece in enumerate(pieces):
            cols = pl.ds(h * PAIR * HEAD_DIM, PAIR * HEAD_DIM)
            for part, src in enumerate((k, v)):
                to = pl.ds(part * PAIR * HEAD_DIM, PAIR * HEAD_DIM)
                block = src.at[rows, cols]
                copies.append((block, piece.at[pl.ds(0, HALF), to]))
                if role == 0:
                    copies.append((block, fz.at[pl.ds(h * HALF, HALF), to]))
    copies = [
        pltpu.make_async_copy(src, dst, sem.at[i]) for i, (src, dst) in enumerate(copies)
    ]
    for copy in copies:
        copy.start()
    for role, piece in enumerate((f1, b1)):
        row = ids[:, role * HALF : (role + 1) * HALF].astype(jnp.float32) + 1.0
        row = jnp.broadcast_to(row, (8, HALF)).astype(jnp.bfloat16)
        piece[HALF : HALF + 8, :] = row
        if role == 0:
            fz[2 * HALF : 2 * HALF + 8, :] = row
    for copy in copies:
        copy.wait()


def pack(k, v, ids):
    def shape(rows):
        return jax.ShapeDtypeStruct((rows, HALF), jnp.bfloat16)

    return pl.pallas_call(
        pack_kernel,
        out_shape=(
            shape(HALF + 8),
            shape(HALF),
            shape(2 * HALF + 8),
            shape(HALF + 8),
            shape(HALF),
        ),
        in_specs=[HBM, HBM, VMEM],
        out_specs=[VMEM] * 5,
        scratch_shapes=[pltpu.SemaphoreType.DMA((12,))],
        compiler_params=PARAMS,
        cost_estimate=pl.CostEstimate(
            flops=1 << 20, bytes_accessed=6 << 20, transcendentals=0
        ),
        name="pack",
    )(k, v, ids)


def stacked_queries(q, rows, first_head):
    return jnp.concatenate(
        [q[rows, head_cols(first_head + j)] for j in range(GROUPS)], axis=0
    )


def near_kernel(h, n, idx, q, k, v, sq, ids, zp, za, pa, zm, piece, acc, mx, ls):
    from_partner = idx[0] >= n - 2
    own_seg = ids[...].astype(jnp.float32) + 1.0
    for role in range(2):
        base = role * HALF
        seg_far = zp[2 * HALF : 2 * HALF + 1, :]
        if role == 1:
            seg_far = jnp.where(
                from_partner, pa[HALF : HALF + 1, :], za[HALF : HALF + 1, :]
            )
        seg_far = seg_far.astype(jnp.float32)
        for g in range(PAIR):
            kcol = head_cols(g)
            vcol = head_cols(PAIR + g)
            own = head_cols(PAIR * h + g)
            far_rows = slice(h * HALF, (h + 1) * HALF)
            if role == 0:
                k_far = zp[far_rows, kcol]
                v_far = zp[far_rows, vcol]
            else:
                k_far = jnp.where(from_partner, piece[0:HALF, kcol], zm[0:HALF, kcol])
                v_far = jnp.where(from_partner, piece[0:HALF, vcol], zm[0:HALF, vcol])
            for i in range(HALF // TILE):
                rows = slice(base + i * TILE, base + (i + 1) * TILE)
                q2 = stacked_queries(q, rows, (PAIR * h + g) * GROUPS)
                n_own = (i + 1) * TILE
                s_own = dot_nt(q2, k[base : base + n_own, own])
                s_far = dot_nt(q2, k_far[i * TILE :])
                seg_q = sq[rows, :]
                see_own = same_segment(seg_q, own_seg[:, base : base + n_own])
                see_far = same_segment(seg_q, seg_far[:, i * TILE :])
                r = lax.broadcasted_iota(jnp.int32, see_own.shape, 0) + i * TILE
                c = lax.broadcasted_iota(jnp.int32, see_own.shape, 1)
                see_own = see_own & (c <= r)
                r = lax.broadcasted_iota(jnp.int32, see_far.shape, 0)
                c = lax.broadcasted_iota(jnp.int32, see_far.shape, 1)
                see_far = see_far & (c > r)
                s_own = jnp.where(jnp.concatenate([see_own] * GROUPS, axis=0), s_own, HIDDEN)
                s_far = jnp.where(jnp.concatenate([see_far] * GROUPS, axis=0), s_far, HIDDEN)
                m = jnp.maximum(
                    jnp.max(s_own, axis=-1, keepdims=True),
                    jnp.max(s_far, axis=-1, keepdims=True),
                )
                p_own = jnp.exp2((s_own - m) * EXP_SCALE)
                p_far = jnp.exp2((s_far - m) * EXP_SCALE)
                part = lane_sum(p_own) + lane_sum(p_far)
                o = dot_nn(p_own.astype(jnp.bfloat16), v[base : base + n_own, own])
                o = o + dot_nn(p_far.astype(jnp.bfloat16), v_far[i * TILE :])
                m = jnp.broadcast_to(m, part.shape)
                for j in range(GROUPS):
                    col = head_cols(GROUPS * g + j)
                    mine = slice(j * TILE, (j + 1) * TILE)
                    acc[rows, col] = o[mine]
                    mx[rows, col] = m[mine]
                    ls[rows, col] = part[mine]


def near(h, n, idx, q, k, v, sq, ids, zp, za, pa, zm, piece):
    state = jax.ShapeDtypeStruct((2 * HALF, 2 * PAIR * HEAD_DIM), jnp.float32)
    return pl.pallas_call(
        functools.partial(near_kernel, h, n),
        out_shape=(state,) * 3,
        in_specs=[SMEM] + [VMEM] * 10,
        out_specs=[VMEM] * 3,
        compiler_params=PARAMS,
        cost_estimate=pl.CostEstimate(
            flops=3 << 30, bytes_accessed=12 << 20, transcendentals=3 << 20
        ),
    )(idx, q, k, v, sq, ids, zp, za, pa, zm, piece)


def last_kernel(h, role, n, idx, q, sq, alt_a, alt_b, alt_seg, kv, kv_seg, acc, mx, ls, *rest):
    out, o_buf, sem = rest[-3:]
    base = role * HALF
    if role == 0:
        use_alt = idx[0] % 2 == 1
        seg = jnp.where(use_alt, alt_seg[HALF : HALF + 1, :], kv_seg[HALF : HALF + 1, :])
        seg = seg.astype(jnp.float32)
    else:
        use_alt = idx[0] == n - 1
        seg = jnp.where(
            use_alt,
            alt_seg[:, 0:HALF].astype(jnp.float32) + 1.0,
            kv_seg[HALF : HALF + 1, :].astype(jnp.float32),
        )
    for g in range(PAIR):
        if role == 0:
            k_alt = alt_a[0:HALF, head_cols(g)]
            v_alt = alt_a[0:HALF, head_cols(PAIR + g)]
        else:
            k_alt = alt_a[0:HALF, head_cols(PAIR * h + g)]
            v_alt = alt_b[0:HALF, head_cols(PAIR * h + g)]
        k_mid = jnp.where(use_alt, k_alt, kv[0:HALF, head_cols(g)])
        v_mid = jnp.where(use_alt, v_alt, kv[0:HALF, head_cols(PAIR + g)])
        for i in range(HALF // TILE):
            rows = slice(base + i * TILE, base + (i + 1) * TILE)
            q2 = stacked_queries(q, rows, (PAIR * h + g) * GROUPS)
            s = dot_nt(q2, k_mid)
            see = same_segment(sq[rows, :], seg)
            s = jnp.where(jnp.concatenate([see] * GROUPS, axis=0), s, HIDDEN)
            cols = [head_cols(GROUPS * g + j) for j in range(GROUPS)]
            m_old = jnp.concatenate([mx[rows, c] for c in cols], axis=0)
            l_old = jnp.concatenate([ls[rows, c] for c in cols], axis=0)
            a_old = jnp.concatenate([acc[rows, c] for c in cols], axis=0)
            m = jnp.maximum(m_old, jnp.max(s, axis=-1, keepdims=True))
            keep = jnp.exp2((m_old - m) * EXP_SCALE)
            p = jnp.exp2((s - jnp.concatenate([m] * (HALF // HEAD_DIM), axis=1)) * EXP_SCALE)
            total = jnp.sum(keep * l_old + lane_sum(p), axis=-1, keepdims=True)
            o = keep * a_old + dot_nn(p.astype(jnp.bfloat16), v_mid)
            o = (o * (1.0 / total)).astype(jnp.bfloat16)
            for j in range(GROUPS):
                o_buf[i * TILE : (i + 1) * TILE, cols[j]] = o[j * TILE : (j + 1) * TILE]
    width = 2 * PAIR * HEAD_DIM
    copy = pltpu.make_async_copy(
        o_buf, out.at[pl.ds(base, HALF), pl.ds(h * width, width)], sem
    )
    copy.start()
    copy.wait()


def last(h, role, n, idx, q, sq, alt_a, alt_b, alt_seg, kv, kv_seg, state, out):
    args = (idx, q, sq, alt_a, alt_b, alt_seg, kv, kv_seg) + state
    aliases = {}
    specs = [SMEM] + [VMEM] * (len(args) - 1)
    if out is not None:
        aliases = {len(args): 0}
        args = args + (out,)
        specs.append(ANY)
    return pl.pallas_call(
        functools.partial(last_kernel, h, role, n),
        out_shape=jax.ShapeDtypeStruct(q.shape, q.dtype),
        in_specs=specs,
        out_specs=ANY,
        input_output_aliases=aliases,
        scratch_shapes=[
            pltpu.VMEM((HALF, 2 * PAIR * HEAD_DIM), jnp.bfloat16),
            pltpu.SemaphoreType.DMA,
        ],
        compiler_params=PARAMS,
        cost_estimate=pl.CostEstimate(
            flops=1 << 30, bytes_accessed=5 << 20, transcendentals=1 << 20
        ),
    )(*args)


def body(queries, key_states, value_states, segment_ids):
    n = lax.axis_size("seq")
    seq = lax.axis_index("seq").astype(jnp.int32)
    idx = seq.reshape(1)
    ids = segment_ids.reshape(1, 2 * HALF)
    sq = jnp.broadcast_to(segment_ids.astype(jnp.float32)[:, None] + 1.0, (2 * HALF, HEAD_DIM))

    partner = [(i, i ^ 1) for i in range(n)]
    up_two = [(i, i + 2) for i in range(n - 2)]
    down_two = [(i + 2, i) for i in range(n - 2)]
    relay = [(i, i + 2) for i in range(0, n - 2, 2)]

    def send(x, route):
        return lax.ppermute(x, "seq", route)

    f1, f2, fz, b1, b2 = pack(
        pltpu.with_memory_space_constraint(key_states, pltpu.HBM),
        pltpu.with_memory_space_constraint(value_states, pltpu.HBM),
        ids,
    )
    pa = send(f1, partner)
    zp = send(fz, up_two)
    za = send(b1, down_two)
    pb = send(f2, partner)
    zb = send(b2, down_two)
    r1 = send(pa, relay)
    even = seq % 2 == 0
    back = jnp.where(even, za, b1)
    d1 = send(back, partner)
    r2 = send(pb, relay)
    back = jnp.where(even, zb, b2)
    d2 = send(back, partner)

    q, k, v = queries, key_states, value_states
    state1 = tuple(near(0, n, idx, q, k, v, sq, ids, zp, za, pa, za, pa))
    state2 = tuple(near(1, n, idx, q, k, v, sq, ids, zp, za, pa, zb, pb))
    out = last(0, 0, n, idx, q, sq, pa, pa, pa, r1, r1, state1, None)
    out = last(0, 1, n, idx, q, sq, k, v, ids, d1, d1, state1, out)
    out = last(1, 1, n, idx, q, sq, k, v, ids, d2, d1, state2, out)
    out = last(1, 0, n, idx, q, sq, pb, pb, pa, r2, r1, state2, out)
    return out


def solution(mesh):
    in_specs = (
        P(("grp", "seq"), "head"),
        P(("grp", "seq"), "head"),
        P(("grp", "seq"), "head"),
        P(("grp", "seq")),
    )
    out_specs = P(("grp", "seq"), "head")
    return jax.shard_map(body, mesh=mesh, in_specs=in_specs, out_specs=out_specs, check_vma=False)
```

```python
import functools
import math

import jax
import jax.numpy as jnp
from jax import lax
from jax.experimental import pallas as pl
from jax.experimental.pallas import tpu as pltpu
from jax.sharding import PartitionSpec as P

HEAD_DIM = 128
GROUPS = 2
HALF = 512
PAIR = 2
TILE = 256

EXP_SCALE = 168.0 ** (-0.5) * math.log2(math.e)
HIDDEN = -1e30
MATCH = 12288.0

VMEM = pl.BlockSpec(memory_space=pltpu.VMEM)
SMEM = pl.BlockSpec(memory_space=pltpu.SMEM)
ANY = pl.BlockSpec(memory_space=pl.ANY)
HBM = pl.BlockSpec(memory_space=pltpu.HBM)
PARAMS = pltpu.CompilerParams(vmem_limit_bytes=24 << 20)


def dot_nt(a, b):
    return lax.dot_general(
        a, b, (((1,), (1,)), ((), ())), preferred_element_type=jnp.float32
    )


def dot_nn(a, b):
    return lax.dot_general(
        a, b, (((1,), (0,)), ((), ())), preferred_element_type=jnp.float32
    )


def head_cols(head):
    return slice(head * HEAD_DIM, (head + 1) * HEAD_DIM)


def pack_kernel(k, v, ids, f1, f2, fz, b1, b2, row8, ids_v, sem):
    get_ids = pltpu.make_async_copy(ids, ids_v, sem.at[12])
    get_ids.start()
    copies = []
    for role, pieces in enumerate(((f1, f2), (b1, b2))):
        rows = pl.ds(role * HALF, HALF)
        for h, piece in enumerate(pieces):
            cols = pl.ds(h * PAIR * HEAD_DIM, PAIR * HEAD_DIM)
            for part, src in enumerate((k, v)):
                to = pl.ds(part * PAIR * HEAD_DIM, PAIR * HEAD_DIM)
                block = src.at[rows, cols]
                copies.append((block, piece.at[pl.ds(0, HALF), to]))
                if role == 0:
                    copies.append((block, fz.at[pl.ds(h * HALF, HALF), to]))
    copies = [
        pltpu.make_async_copy(src, dst, sem.at[i]) for i, (src, dst) in enumerate(copies)
    ]
    for copy in copies:
        copy.start()
    get_ids.wait()
    row = jnp.broadcast_to(ids_v[...].astype(jnp.float32) + 1.0, (8, 2 * HALF))
    row = row.astype(jnp.bfloat16)
    row8[...] = row
    f1[HALF : HALF + 8, :] = row[:, :HALF]
    fz[2 * HALF : 2 * HALF + 8, :] = row[:, :HALF]
    b1[HALF : HALF + 8, :] = row[:, HALF:]
    for copy in copies:
        copy.wait()


def pack(k, v, ids):
    def shape(rows, cols=HALF):
        return jax.ShapeDtypeStruct((rows, cols), jnp.bfloat16)

    return pl.pallas_call(
        pack_kernel,
        out_shape=(
            shape(HALF + 8),
            shape(HALF),
            shape(2 * HALF + 8),
            shape(HALF + 8),
            shape(HALF),
            shape(8, 2 * HALF),
        ),
        in_specs=[HBM, HBM, HBM],
        out_specs=[VMEM] * 6,
        scratch_shapes=[
            pltpu.VMEM((1, 2 * HALF), jnp.int32),
            pltpu.SemaphoreType.DMA((13,)),
        ],
        compiler_params=PARAMS,
        cost_estimate=pl.CostEstimate(
            flops=1 << 20, bytes_accessed=6 << 20, transcendentals=0
        ),
        name="pack",
    )(k, v, ids)


def one_hot_keys(row):
    lane = lax.broadcasted_iota(jnp.int32, (HEAD_DIM, HALF), 0).astype(jnp.float32)
    hot = jnp.where(lane == row.astype(jnp.float32), 1.0, 0.0)
    return hot.T.astype(jnp.bfloat16)


def stacked_queries(q, hot, rows, first_head):
    mark = hot[rows, :] * jnp.bfloat16(MATCH)
    return jnp.concatenate(
        [
            jnp.concatenate([q[rows, head_cols(first_head + j)], mark], axis=1)
            for j in range(GROUPS)
        ],
        axis=0,
    )


def with_ones(v):
    return jnp.concatenate([v, jnp.ones(v.shape, v.dtype)], axis=1)


def near_kernel(
    h, n, idx, q, k, v, hot, zp, za, pa, zm, piece, acc, mx, ls, far, seg, sem
):
    from_partner = idx[0] >= n - 2
    body_rows = pl.ds(0, HALF)
    id_rows = pl.ds(HALF, 8)
    copies = [
        pltpu.make_async_copy(zp.at[pl.ds(2 * HALF, 8)], seg.at[0], sem.at[0]),
        pltpu.make_async_copy(zp.at[pl.ds(h * HALF, HALF)], far.at[0], sem.at[1]),
        pltpu.make_async_copy(za.at[id_rows], seg.at[1], sem.at[2]),
        pltpu.make_async_copy(zm.at[body_rows], far.at[1], sem.at[3]),
    ]
    copies[0].start()
    copies[1].start()

    @pl.when(from_partner)
    def _():
        pltpu.make_async_copy(pa.at[id_rows], seg.at[1], sem.at[2]).start()
        pltpu.make_async_copy(piece.at[body_rows], far.at[1], sem.at[3]).start()

    @pl.when(jnp.logical_not(from_partner))
    def _():
        copies[2].start()
        copies[3].start()

    for role in range(2):
        base = role * HALF
        copies[2 * role].wait()
        hot_far = one_hot_keys(seg[role, 0:1, :])
        copies[2 * role + 1].wait()
        for g in range(PAIR):
            own = head_cols(PAIR * h + g)
            k_far = jnp.concatenate([far[role, :, head_cols(g)], hot_far], axis=1)
            v_far = with_ones(far[role, :, head_cols(PAIR + g)])
            for i in range(HALF // TILE):
                rows = slice(base + i * TILE, base + (i + 1) * TILE)
                q2 = stacked_queries(q, hot, rows, (PAIR * h + g) * GROUPS)
                n_own = (i + 1) * TILE
                seen = slice(base, base + n_own)
                k_own = jnp.concatenate([k[seen, own], hot[seen, :]], axis=1)
                s_own = dot_nt(q2, k_own)
                s_far = dot_nt(q2, k_far[i * TILE :])
                r = lax.broadcasted_iota(jnp.int32, (TILE, TILE), 0)
                c = lax.broadcasted_iota(jnp.int32, (TILE, TILE), 1)
                below = jnp.concatenate([c <= r] * GROUPS, axis=0)
                above = jnp.concatenate([c > r] * GROUPS, axis=0)
                edge = jnp.where(below, s_own[:, n_own - TILE :], HIDDEN)
                if i > 0:
                    edge = jnp.concatenate([s_own[:, : n_own - TILE], edge], axis=1)
                s_own = edge
                edge = jnp.where(above, s_far[:, :TILE], HIDDEN)
                if (i + 1) * TILE < HALF:
                    edge = jnp.concatenate([edge, s_far[:, TILE:]], axis=1)
                s_far = edge
                m = jnp.maximum(
                    jnp.max(s_own, axis=-1, keepdims=True),
                    jnp.max(s_far, axis=-1, keepdims=True),
                )
                p_own = jnp.exp2((s_own - m) * EXP_SCALE).astype(jnp.bfloat16)
                p_far = jnp.exp2((s_far - m) * EXP_SCALE).astype(jnp.bfloat16)
                o = dot_nn(p_own, with_ones(v[seen, own]))
                o = o + dot_nn(p_far, v_far[i * TILE :])
                m = jnp.broadcast_to(m, (GROUPS * TILE, HEAD_DIM))
                for j in range(GROUPS):
                    col = head_cols(GROUPS * g + j)
                    mine = slice(j * TILE, (j + 1) * TILE)
                    acc[rows, col] = o[mine, :HEAD_DIM]
                    mx[rows, col] = m[mine]
                    ls[rows, col] = o[mine, HEAD_DIM:]


def near(h, n, idx, q, k, v, hot, zp, za, pa, zm, piece):
    state = jax.ShapeDtypeStruct((2 * HALF, 2 * PAIR * HEAD_DIM), jnp.float32)
    return pl.pallas_call(
        functools.partial(near_kernel, h, n),
        out_shape=(state,) * 3,
        in_specs=[SMEM] + [VMEM] * 4 + [ANY] * 5,
        out_specs=[VMEM] * 3,
        scratch_shapes=[
            pltpu.VMEM((2, HALF, HALF), jnp.bfloat16),
            pltpu.VMEM((2, 8, HALF), jnp.bfloat16),
            pltpu.SemaphoreType.DMA((4,)),
        ],
        compiler_params=PARAMS,
        cost_estimate=pl.CostEstimate(
            flops=3 << 30, bytes_accessed=12 << 20, transcendentals=3 << 20
        ),
    )(idx, q, k, v, hot, zp, za, pa, zm, piece)


def last_kernel(h, role, n, idx, q, hot, alts, alt_seg, kv, kv_seg, acc, mx, ls, *rest):
    out, mid, seg, o_buf, sem, out_sem = rest[-6:]
    base = role * HALF
    width = PAIR * HEAD_DIM
    body_rows = pl.ds(0, HALF)
    k_mid = mid.at[:, pl.ds(0, width)]
    v_mid = mid.at[:, pl.ds(width, width)]
    copies = [
        pltpu.make_async_copy(kv_seg.at[pl.ds(HALF, 8)], seg, sem.at[0]),
        pltpu.make_async_copy(kv.at[body_rows, pl.ds(0, width)], k_mid, sem.at[1]),
        pltpu.make_async_copy(kv.at[body_rows, pl.ds(width, width)], v_mid, sem.at[2]),
    ]
    if role == 0:
        use_alt = idx[0] % 2 == 1
        (piece,) = alts
        others = (
            alt_seg.at[pl.ds(HALF, 8)],
            piece.at[body_rows, pl.ds(0, width)],
            piece.at[body_rows, pl.ds(width, width)],
        )
    else:
        use_alt = idx[0] == n - 1
        own = pl.ds(h * width, width)
        others = (alt_seg.at[:, body_rows],) + tuple(a.at[body_rows, own] for a in alts)

    @pl.when(use_alt)
    def _():
        for i, (src, dst) in enumerate(zip(others, (seg, k_mid, v_mid))):
            pltpu.make_async_copy(src, dst, sem.at[i]).start()

    @pl.when(jnp.logical_not(use_alt))
    def _():
        for copy in copies:
            copy.start()

    copies[0].wait()
    hot_mid = one_hot_keys(seg[0:1, :])
    copies[1].wait()
    sends = []
    for g in range(PAIR):
        k_aug = jnp.concatenate([mid[:, head_cols(g)], hot_mid], axis=1)
        for i in range(HALF // TILE):
            rows = slice(base + i * TILE, base + (i + 1) * TILE)
            q2 = stacked_queries(q, hot, rows, (PAIR * h + g) * GROUPS)
            s = dot_nt(q2, k_aug)
            if g == 0 and i == 0:
                copies[2].wait()
            v_aug = with_ones(mid[:, head_cols(PAIR + g)])
            cols = [head_cols(GROUPS * g + j) for j in range(GROUPS)]
            m_old = jnp.concatenate([mx[rows, c] for c in cols], axis=0)
            l_old = jnp.concatenate([ls[rows, c] for c in cols], axis=0)
            a_old = jnp.concatenate([acc[rows, c] for c in cols], axis=0)
            m = jnp.maximum(m_old, jnp.max(s, axis=-1, keepdims=True))
            keep = jnp.exp2((m_old - m) * EXP_SCALE)
            p = jnp.exp2((s - jnp.concatenate([m] * (HALF // HEAD_DIM), axis=1)) * EXP_SCALE)
            o = dot_nn(p.astype(jnp.bfloat16), v_aug)
            total = keep * l_old + o[:, HEAD_DIM:]
            o = (keep * a_old + o[:, :HEAD_DIM]) * (1.0 / total)
            o = o.astype(jnp.bfloat16)
            for j in range(GROUPS):
                o_buf[i * TILE : (i + 1) * TILE, cols[j]] = o[j * TILE : (j + 1) * TILE]
        part = pl.ds(g * GROUPS * HEAD_DIM, GROUPS * HEAD_DIM)
        to = pl.ds((PAIR * h + g) * GROUPS * HEAD_DIM, GROUPS * HEAD_DIM)
        sends.append(
            pltpu.make_async_copy(
                o_buf.at[:, part], out.at[pl.ds(base, HALF), to], out_sem.at[g]
            )
        )
        sends[-1].start()
    for copy in sends:
        copy.wait()


def last(h, role, n, idx, q, hot, alts, alt_seg, kv, kv_seg, state, out):
    n_alt = len(alts)

    def kernel(idx, q, hot, *refs):
        last_kernel(h, role, n, idx, q, hot, refs[:n_alt], *refs[n_alt:])

    args = (idx, q, hot) + alts + (alt_seg, kv, kv_seg) + state
    specs = [SMEM] + [VMEM] * 2 + [ANY] * (n_alt + 3) + [VMEM] * 3
    aliases = {}
    if out is not None:
        aliases = {len(args): 0}
        args = args + (out,)
        specs.append(ANY)
    return pl.pallas_call(
        kernel,
        out_shape=jax.ShapeDtypeStruct(q.shape, q.dtype),
        in_specs=specs,
        out_specs=ANY,
        input_output_aliases=aliases,
        scratch_shapes=[
            pltpu.VMEM((HALF, HALF), jnp.bfloat16),
            pltpu.VMEM((8, HALF), jnp.bfloat16),
            pltpu.VMEM((HALF, 2 * PAIR * HEAD_DIM), jnp.bfloat16),
            pltpu.SemaphoreType.DMA((3,)),
            pltpu.SemaphoreType.DMA((PAIR,)),
        ],
        compiler_params=PARAMS,
        cost_estimate=pl.CostEstimate(
            flops=1 << 30, bytes_accessed=5 << 20, transcendentals=1 << 20
        ),
    )(*args)


def body(queries, key_states, value_states, segment_ids):
    n = lax.axis_size("seq")
    seq = lax.axis_index("seq").astype(jnp.int32)
    idx = seq.reshape(1)
    lane = jnp.arange(HEAD_DIM, dtype=jnp.int32)
    hot = (segment_ids[:, None] + 1 == lane[None, :]).astype(jnp.bfloat16)

    partner = [(i, i ^ 1) for i in range(n)]
    up_two = [(i, i + 2) for i in range(n - 2)]
    down_two = [(i + 2, i) for i in range(n - 2)]
    relay = [(i, i + 2) for i in range(0, n - 2, 2)]

    def send(x, route):
        return lax.ppermute(x, "seq", route)

    q, k, v = queries, key_states, value_states
    f1, f2, fz, b1, b2, row8 = pack(
        pltpu.with_memory_space_constraint(k, pltpu.HBM),
        pltpu.with_memory_space_constraint(v, pltpu.HBM),
        segment_ids.reshape(1, 2 * HALF),
    )
    pa = send(f1, partner)
    zp = send(fz, up_two)
    za = send(b1, down_two)
    pb = send(f2, partner)
    zb = send(b2, down_two)
    r1 = send(pa, relay)
    even = seq % 2 == 0
    back = jnp.where(even, za, b1)
    d1 = send(back, partner)
    r2 = send(pb, relay)
    back = jnp.where(even, zb, b2)
    d2 = send(back, partner)

    state1 = tuple(near(0, n, idx, q, k, v, hot, zp, za, pa, za, pa))
    state2 = tuple(near(1, n, idx, q, k, v, hot, zp, za, pa, zb, pb))
    out = last(0, 0, n, idx, q, hot, (pa,), pa, r1, r1, state1, None)
    out = last(0, 1, n, idx, q, hot, (k, v), row8, d1, d1, state1, out)
    out = last(1, 1, n, idx, q, hot, (k, v), row8, d2, d1, state2, out)
    out = last(1, 0, n, idx, q, hot, (pb,), pa, r2, r1, state2, out)
    return out


def solution(mesh):
    in_specs = (
        P(("grp", "seq"), "head"),
        P(("grp", "seq"), "head"),
        P(("grp", "seq"), "head"),
        P(("grp", "seq")),
    )
    out_specs = P(("grp", "seq"), "head")
    return jax.shard_map(body, mesh=mesh, in_specs=in_specs, out_specs=out_specs, check_vma=False)
```

```python
import functools
import math

import jax
import jax.numpy as jnp
from jax import lax
from jax.experimental import pallas as pl
from jax.experimental.pallas import tpu as pltpu
from jax.sharding import PartitionSpec as P

HEAD_DIM = 128
GROUPS = 2
HALF = 512
PAIR = 2
TILE = 256
TILES = HALF // TILE

EXP_SCALE = 168.0 ** (-0.5) * math.log2(math.e)
HIDDEN = -1e30
MATCH = 12288.0

VMEM = pl.BlockSpec(memory_space=pltpu.VMEM)
SMEM = pl.BlockSpec(memory_space=pltpu.SMEM)
ANY = pl.BlockSpec(memory_space=pl.ANY)
HBM = pl.BlockSpec(memory_space=pltpu.HBM)
PARAMS = pltpu.CompilerParams(vmem_limit_bytes=24 << 20)


def dot_nt(a, b):
    return lax.dot_general(
        a, b, (((1,), (1,)), ((), ())), preferred_element_type=jnp.float32
    )


def dot_nn(a, b):
    return lax.dot_general(
        a, b, (((1,), (0,)), ((), ())), preferred_element_type=jnp.float32
    )


def head_cols(head):
    return slice(head * HEAD_DIM, (head + 1) * HEAD_DIM)


def pack_kernel(k, v, ids, f1, f2, fz, b1, b2, row8, ids_v, sem):
    get_ids = pltpu.make_async_copy(ids, ids_v, sem.at[12])
    get_ids.start()
    copies = []
    for role, pieces in enumerate(((f1, f2), (b1, b2))):
        rows = pl.ds(role * HALF, HALF)
        for h, piece in enumerate(pieces):
            cols = pl.ds(h * PAIR * HEAD_DIM, PAIR * HEAD_DIM)
            for part, src in enumerate((k, v)):
                to = pl.ds(part * PAIR * HEAD_DIM, PAIR * HEAD_DIM)
                block = src.at[rows, cols]
                copies.append((block, piece.at[pl.ds(0, HALF), to]))
                if role == 0:
                    copies.append((block, fz.at[pl.ds(h * HALF, HALF), to]))
    copies = [
        pltpu.make_async_copy(src, dst, sem.at[i]) for i, (src, dst) in enumerate(copies)
    ]
    for copy in copies:
        copy.start()
    get_ids.wait()
    row = jnp.broadcast_to(ids_v[...].astype(jnp.float32) + 1.0, (8, 2 * HALF))
    row = row.astype(jnp.bfloat16)
    row8[...] = row
    f1[HALF : HALF + 8, :] = row[:, :HALF]
    fz[2 * HALF : 2 * HALF + 8, :] = row[:, :HALF]
    b1[HALF : HALF + 8, :] = row[:, HALF:]
    for copy in copies:
        copy.wait()


def pack(k, v, ids):
    def shape(rows, cols=HALF):
        return jax.ShapeDtypeStruct((rows, cols), jnp.bfloat16)

    return pl.pallas_call(
        pack_kernel,
        out_shape=(
            shape(HALF + 8),
            shape(HALF),
            shape(2 * HALF + 8),
            shape(HALF + 8),
            shape(HALF),
            shape(8, 2 * HALF),
        ),
        in_specs=[HBM, HBM, HBM],
        out_specs=[VMEM] * 6,
        scratch_shapes=[
            pltpu.VMEM((1, 2 * HALF), jnp.int32),
            pltpu.SemaphoreType.DMA((13,)),
        ],
        compiler_params=PARAMS,
        cost_estimate=pl.CostEstimate(
            flops=1 << 20, bytes_accessed=6 << 20, transcendentals=0
        ),
        name="pack",
    )(k, v, ids)


def one_hot_keys(row):
    lane = lax.broadcasted_iota(jnp.int32, (HEAD_DIM, HALF), 0).astype(jnp.float32)
    hot = jnp.where(lane == row.astype(jnp.float32), 1.0, 0.0)
    return hot.T.astype(jnp.bfloat16)


def stacked_queries(q, hot, base, first_head):
    blocks = []
    for i in range(TILES):
        rows = slice(base + i * TILE, base + (i + 1) * TILE)
        mark = hot[rows, :] * jnp.bfloat16(MATCH)
        for j in range(GROUPS):
            blocks.append(jnp.concatenate([q[rows, head_cols(first_head + j)], mark], axis=1))
    return jnp.concatenate(blocks, axis=0)


def with_ones(v):
    return jnp.concatenate([v, jnp.ones(v.shape, v.dtype)], axis=1)


def tile_rows(x, i):
    return x[i * GROUPS * TILE : (i + 1) * GROUPS * TILE]


def edge_mask(above):
    r = lax.broadcasted_iota(jnp.int32, (TILE, TILE), 0)
    c = lax.broadcasted_iota(jnp.int32, (TILE, TILE), 1)
    return jnp.concatenate([c > r if above else c <= r] * GROUPS, axis=0)


def triangle_scores(q2, k_aug, above):
    mask = edge_mask(above)
    seen = [[] for _ in range(TILES)]
    for t in range(TILES):
        first, end = (0, t + 1) if above else (t, TILES)
        rows = q2[first * GROUPS * TILE : end * GROUPS * TILE]
        s = dot_nt(rows, k_aug[t * TILE : (t + 1) * TILE])
        for i in range(first, end):
            part = tile_rows(s, i - first)
            if i == t:
                part = jnp.where(mask, part, HIDDEN)
            seen[i].append(part)
    return seen


def triangle_values(probs, v_aug, above):
    total = [None] * TILES
    for t in range(TILES):
        first, end = (0, t + 1) if above else (t, TILES)
        rows = jnp.concatenate(
            [probs[i][t - i if above else t] for i in range(first, end)], axis=0
        )
        o = dot_nn(rows, v_aug[t * TILE : (t + 1) * TILE])
        for i in range(first, end):
            part = tile_rows(o, i - first)
            total[i] = part if total[i] is None else total[i] + part
    return total


def row_max(parts):
    top = parts[0]
    for part in parts[1:]:
        top = jnp.maximum(top, part)
    return jnp.max(top, axis=-1, keepdims=True)


def weights(parts, m):
    wide = jnp.concatenate([m] * (TILE // HEAD_DIM), axis=1)
    return [jnp.exp2((part - wide) * EXP_SCALE).astype(jnp.bfloat16) for part in parts]


def state_slices(base, g):
    for i in range(TILES):
        for j in range(GROUPS):
            rows = slice(base + i * TILE, base + (i + 1) * TILE)
            yield i, slice(j * TILE, (j + 1) * TILE), rows, head_cols(GROUPS * g + j)


def load_state(ref, base, g):
    parts = [[] for _ in range(TILES)]
    for i, _, rows, cols in state_slices(base, g):
        parts[i].append(ref[rows, cols])
    return [jnp.concatenate(p, axis=0) for p in parts]


def own_kernel(h, q, k, v, hot, acc, mx, ls):
    for role in range(2):
        base = role * HALF
        seen = slice(base, base + HALF)
        for g in range(PAIR):
            own = head_cols(PAIR * h + g)
            q2 = stacked_queries(q, hot, base, (PAIR * h + g) * GROUPS)
            k_aug = jnp.concatenate([k[seen, own], hot[seen, :]], axis=1)
            scores = triangle_scores(q2, k_aug, False)
            tops = [
                jnp.broadcast_to(row_max(parts), (GROUPS * TILE, HEAD_DIM)) for parts in scores
            ]
            probs = [weights(parts, m) for parts, m in zip(scores, tops)]
            o = triangle_values(probs, with_ones(v[seen, own]), False)
            for i, mine, rows, cols in state_slices(base, g):
                acc[rows, cols] = o[i][mine, :HEAD_DIM]
                ls[rows, cols] = o[i][mine, HEAD_DIM:]
                mx[rows, cols] = tops[i][mine]


STATE = jax.ShapeDtypeStruct((2 * HALF, 2 * PAIR * HEAD_DIM), jnp.float32)


def cost(gflop):
    return pl.CostEstimate(
        flops=gflop << 30, bytes_accessed=8 << 20, transcendentals=2 << 20
    )


def own(h, q, k, v, hot):
    return pl.pallas_call(
        functools.partial(own_kernel, h),
        out_shape=(STATE,) * 3,
        in_specs=[VMEM] * 4,
        out_specs=[VMEM] * 3,
        compiler_params=PARAMS,
        cost_estimate=cost(2),
    )(q, k, v, hot)


def far_kernel(h, n, idx, q, hot, zp, za, pa, zm, piece, acc0, mx0, ls0, acc, mx, ls):
    from_partner = idx[0] >= n - 2
    for role in range(2):
        base = role * HALF
        if role == 0:
            seg = zp[2 * HALF : 2 * HALF + 1, :]
            far = zp[h * HALF : (h + 1) * HALF, :]
        else:
            seg = jnp.where(from_partner, pa[HALF : HALF + 1, :], za[HALF : HALF + 1, :])
            far = jnp.where(from_partner, piece[0:HALF, :], zm[0:HALF, :])
        hot_far = one_hot_keys(seg)
        for g in range(PAIR):
            q2 = stacked_queries(q, hot, base, (PAIR * h + g) * GROUPS)
            k_aug = jnp.concatenate([far[:, head_cols(g)], hot_far], axis=1)
            scores = triangle_scores(q2, k_aug, True)
            old = load_state(mx0, base, g)
            tops = [jnp.maximum(m, row_max(parts)) for m, parts in zip(old, scores)]
            probs = [weights(parts, m) for parts, m in zip(scores, tops)]
            o = triangle_values(probs, with_ones(far[:, head_cols(PAIR + g)]), True)
            for i, mine, rows, cols in state_slices(base, g):
                keep = jnp.exp2((old[i][mine] - tops[i][mine]) * EXP_SCALE)
                acc[rows, cols] = keep * acc0[rows, cols] + o[i][mine, :HEAD_DIM]
                ls[rows, cols] = keep * ls0[rows, cols] + o[i][mine, HEAD_DIM:]
                mx[rows, cols] = tops[i][mine]


def far(h, n, idx, q, hot, zp, za, pa, zm, piece, state):
    return pl.pallas_call(
        functools.partial(far_kernel, h, n),
        out_shape=(STATE,) * 3,
        in_specs=[SMEM] + [VMEM] * 10,
        out_specs=[VMEM] * 3,
        compiler_params=PARAMS,
        cost_estimate=cost(2),
    )(idx, q, hot, zp, za, pa, zm, piece, *state)


def last_kernel(
    h, n, idx, q, hot, k, v, row8, pa, piece, r1, relayed, d1, back, acc, mx, ls, *rest
):
    out, o_buf, sem = rest[-3:]
    odd = idx[0] % 2 == 1
    end = idx[0] == n - 1
    width = PAIR * HEAD_DIM
    mine_cols = slice(h * width, (h + 1) * width)
    sends = []
    for role in range(2):
        base = role * HALF
        if role == 0:
            seg = jnp.where(odd, pa[HALF : HALF + 1, :], r1[HALF : HALF + 1, :])
            k_mid = jnp.where(odd, piece[0:HALF, :width], relayed[0:HALF, :width])
            v_mid = jnp.where(odd, piece[0:HALF, width:], relayed[0:HALF, width:])
        else:
            seg = jnp.where(end, row8[0:1, :HALF], d1[HALF : HALF + 1, :])
            k_mid = jnp.where(end, k[0:HALF, mine_cols], back[0:HALF, :width])
            v_mid = jnp.where(end, v[0:HALF, mine_cols], back[0:HALF, width:])
        hot_mid = one_hot_keys(seg)
        for g in range(PAIR):
            q2 = stacked_queries(q, hot, base, (PAIR * h + g) * GROUPS)
            k_aug = jnp.concatenate([k_mid[:, head_cols(g)], hot_mid], axis=1)
            s = dot_nt(q2, k_aug)
            old = jnp.concatenate(load_state(mx, base, g), axis=0)
            m = jnp.maximum(old, jnp.max(s, axis=-1, keepdims=True))
            keep = jnp.exp2((old - m) * EXP_SCALE)
            wide = jnp.concatenate([m] * (HALF // HEAD_DIM), axis=1)
            p = jnp.exp2((s - wide) * EXP_SCALE).astype(jnp.bfloat16)
            o = dot_nn(p, with_ones(v_mid[:, head_cols(g)]))
            for i, mine, rows, cols in state_slices(base, g):
                o_i, keep_i = tile_rows(o, i)[mine], tile_rows(keep, i)[mine]
                total = keep_i * ls[rows, cols] + o_i[:, HEAD_DIM:]
                value = keep_i * acc[rows, cols] + o_i[:, :HEAD_DIM]
                o_buf[rows, cols] = (value * (1.0 / total)).astype(jnp.bfloat16)
            part = pl.ds(g * GROUPS * HEAD_DIM, GROUPS * HEAD_DIM)
            to = pl.ds((PAIR * h + g) * GROUPS * HEAD_DIM, GROUPS * HEAD_DIM)
            here = pl.ds(base, HALF)
            sends.append(
                pltpu.make_async_copy(
                    o_buf.at[here, part], out.at[here, to], sem.at[PAIR * role + g]
                )
            )
            sends[-1].start()
    for copy in sends:
        copy.wait()


def last(h, n, idx, q, hot, k, v, row8, pa, piece, r1, relayed, d1, back, state, out):
    args = (idx, q, hot, k, v, row8, pa, piece, r1, relayed, d1, back) + state
    specs = [SMEM] + [VMEM] * (len(args) - 1)
    aliases = {}
    if out is not None:
        aliases = {len(args): 0}
        args = args + (out,)
        specs.append(ANY)
    return pl.pallas_call(
        functools.partial(last_kernel, h, n),
        out_shape=jax.ShapeDtypeStruct(q.shape, q.dtype),
        in_specs=specs,
        out_specs=ANY,
        input_output_aliases=aliases,
        scratch_shapes=[
            pltpu.VMEM((2 * HALF, 2 * PAIR * HEAD_DIM), jnp.bfloat16),
            pltpu.SemaphoreType.DMA((2 * PAIR,)),
        ],
        compiler_params=PARAMS,
        cost_estimate=cost(2),
    )(*args)


def body(queries, key_states, value_states, segment_ids):
    n = lax.axis_size("seq")
    seq = lax.axis_index("seq").astype(jnp.int32)
    idx = seq.reshape(1)
    lane = jnp.arange(HEAD_DIM, dtype=jnp.int32)
    hot = (segment_ids[:, None] + 1 == lane[None, :]).astype(jnp.bfloat16)

    partner = [(i, i ^ 1) for i in range(n)]
    up_two = [(i, i + 2) for i in range(n - 2)]
    down_two = [(i + 2, i) for i in range(n - 2)]
    relay = [(i, i + 2) for i in range(0, n - 2, 2)]

    def send(x, route):
        return lax.ppermute(x, "seq", route)

    q, k, v = queries, key_states, value_states
    f1, f2, fz, b1, b2, row8 = pack(
        pltpu.with_memory_space_constraint(k, pltpu.HBM),
        pltpu.with_memory_space_constraint(v, pltpu.HBM),
        pltpu.with_memory_space_constraint(segment_ids.reshape(1, 2 * HALF), pltpu.HBM),
    )
    pa = send(f1, partner)
    zp = send(fz, up_two)
    za = send(b1, down_two)
    pb = send(f2, partner)
    zb = send(b2, down_two)
    state1 = tuple(own(0, q, k, v, hot))
    r1 = send(pa, relay)
    state2 = tuple(own(1, q, k, v, hot))
    even = seq % 2 == 0
    back = jnp.where(even, za, b1)
    d1 = send(back, partner)
    r2 = send(pb, relay)
    back = jnp.where(even, zb, b2)
    d2 = send(back, partner)

    state1 = tuple(far(0, n, idx, q, hot, zp, za, pa, za, pa, state1))
    state2 = tuple(far(1, n, idx, q, hot, zp, za, pa, zb, pb, state2))
    out = last(0, n, idx, q, hot, k, v, row8, pa, pa, r1, r1, d1, d1, state1, None)
    return last(1, n, idx, q, hot, k, v, row8, pa, pb, r1, r2, d1, d2, state2, out)


def solution(mesh):
    in_specs = (
        P(("grp", "seq"), "head"),
        P(("grp", "seq"), "head"),
        P(("grp", "seq"), "head"),
        P(("grp", "seq")),
    )
    out_specs = P(("grp", "seq"), "head")
    return jax.shard_map(body, mesh=mesh, in_specs=in_specs, out_specs=out_specs, check_vma=False)
```

```python
import functools
import math

import jax
import jax.numpy as jnp
from jax import lax
from jax.experimental import pallas as pl
from jax.experimental.pallas import tpu as pltpu
from jax.sharding import PartitionSpec as P

HEAD_DIM = 128
GROUPS = 2
HALF = 512
PAIR = 2
TILE = 256
TILES = HALF // TILE

EXP_SCALE = 168.0 ** (-0.5) * math.log2(math.e)
HIDDEN = -1e30
MATCH = 12288.0

VMEM = pl.BlockSpec(memory_space=pltpu.VMEM)
SMEM = pl.BlockSpec(memory_space=pltpu.SMEM)
ANY = pl.BlockSpec(memory_space=pl.ANY)
HBM = pl.BlockSpec(memory_space=pltpu.HBM)
PARAMS = pltpu.CompilerParams(vmem_limit_bytes=10 << 20)


def dot_nt(a, b):
    return lax.dot_general(
        a, b, (((1,), (1,)), ((), ())), preferred_element_type=jnp.float32
    )


def dot_nn(a, b):
    return lax.dot_general(
        a, b, (((1,), (0,)), ((), ())), preferred_element_type=jnp.float32
    )


def head_cols(head):
    return slice(head * HEAD_DIM, (head + 1) * HEAD_DIM)


SECOND = HALF + 16
FRONT = SECOND + HALF


def ids_row(ids_v, role):
    row = ids_v[:, role * HALF : (role + 1) * HALF].astype(jnp.float32) + 1.0
    return jnp.broadcast_to(row, (16, HALF)).astype(jnp.bfloat16)


def block_copies(k, v, role, h, target, sem):
    rows = pl.ds(role * HALF, HALF)
    cols = pl.ds(h * PAIR * HEAD_DIM, PAIR * HEAD_DIM)
    return [
        pltpu.make_async_copy(
            src.at[rows, cols],
            target.at[:, pl.ds(part * PAIR * HEAD_DIM, PAIR * HEAD_DIM)],
            sem.at[part],
        )
        for part, src in enumerate((k, v))
    ]


def pack_front_kernel(k, v, ids, f1, front, ids_v, stage, sem, ids_sem, out_sem):
    get_ids = pltpu.make_async_copy(ids, ids_v, ids_sem)
    get_ids.start()
    parts = (pl.ds(0, SECOND), pl.ds(SECOND, HALF))
    copies = [
        block_copies(k, v, 0, h, stage.at[pl.ds(h * SECOND, HALF)], sem.at[h]) for h in range(2)
    ]
    for copy in copies[0] + copies[1]:
        copy.start()
    get_ids.wait()
    stage[HALF:SECOND, :] = ids_row(ids_v, 0)
    first = pl.ds(0, HALF + 8)
    sends = [
        pltpu.make_async_copy(stage.at[first], f1, out_sem.at[0]),
        pltpu.make_async_copy(stage.at[parts[0]], front.at[parts[0]], out_sem.at[1]),
        pltpu.make_async_copy(stage.at[parts[1]], front.at[parts[1]], out_sem.at[2]),
    ]
    for h in range(2):
        for copy in copies[h]:
            copy.wait()
        for send in sends[2 * h : 2 + h]:
            send.start()
    for send in sends:
        send.wait()


def pack_front(k, v, ids):
    return pl.pallas_call(
        pack_front_kernel,
        out_shape=tuple(
            jax.ShapeDtypeStruct((r, HALF), jnp.bfloat16) for r in (HALF + 8, FRONT)
        ),
        in_specs=[HBM] * 3,
        out_specs=[HBM] * 2,
        scratch_shapes=[
            pltpu.VMEM((1, 2 * HALF), jnp.int32),
            pltpu.VMEM((FRONT, HALF), jnp.bfloat16),
            pltpu.SemaphoreType.DMA((2, 2)),
            pltpu.SemaphoreType.DMA,
            pltpu.SemaphoreType.DMA((3,)),
        ],
        compiler_params=PARAMS,
        cost_estimate=pl.CostEstimate(
            flops=1 << 20, bytes_accessed=2 << 20, transcendentals=0
        ),
        name="pack0",
    )(k, v, ids)


def pack_rest_kernel(k, v, ids, b1, f2, b2, ids_v, stage, sem, ids_sem, out_sem):
    get_ids = pltpu.make_async_copy(ids, ids_v, ids_sem)
    get_ids.start()
    pieces = ((1, 0, b1), (0, 1, f2), (1, 1, b2))
    copies = [
        block_copies(k, v, role, h, stage.at[i, pl.ds(0, HALF)], sem.at[i])
        for i, (role, h, _) in enumerate(pieces)
    ]
    for pair in copies:
        for copy in pair:
            copy.start()
    get_ids.wait()
    stage[0, HALF:SECOND, :] = ids_row(ids_v, 1)
    sends = []
    for i, (_, _, piece) in enumerate(pieces):
        for copy in copies[i]:
            copy.wait()
        rows = pl.ds(0, HALF + 8 if i == 0 else HALF)
        sends.append(pltpu.make_async_copy(stage.at[i, rows], piece, out_sem.at[i]))
        sends[-1].start()
    for send in sends:
        send.wait()


def pack_rest(k, v, ids):
    return pl.pallas_call(
        pack_rest_kernel,
        out_shape=tuple(
            jax.ShapeDtypeStruct((r, HALF), jnp.bfloat16) for r in (HALF + 8, HALF, HALF)
        ),
        in_specs=[HBM] * 3,
        out_specs=[HBM] * 3,
        scratch_shapes=[
            pltpu.VMEM((1, 2 * HALF), jnp.int32),
            pltpu.VMEM((3, SECOND, HALF), jnp.bfloat16),
            pltpu.SemaphoreType.DMA((3, 2)),
            pltpu.SemaphoreType.DMA,
            pltpu.SemaphoreType.DMA((3,)),
        ],
        compiler_params=PARAMS,
        cost_estimate=pl.CostEstimate(
            flops=1 << 20, bytes_accessed=3 << 20, transcendentals=0
        ),
        name="pack1",
    )(k, v, ids)


def one_hot_keys(row):
    lane = lax.broadcasted_iota(jnp.int32, (HEAD_DIM, HALF), 0).astype(jnp.float32)
    hot = jnp.where(lane == row.astype(jnp.float32), 1.0, 0.0)
    return hot.T.astype(jnp.bfloat16)


def stacked_queries(q, hot, base, first_head):
    blocks = []
    for i in range(TILES):
        rows = slice(base + i * TILE, base + (i + 1) * TILE)
        mark = hot[rows, :] * jnp.bfloat16(MATCH)
        for j in range(GROUPS):
            blocks.append(jnp.concatenate([q[rows, head_cols(first_head + j)], mark], axis=1))
    return jnp.concatenate(blocks, axis=0)


def with_ones(v):
    return jnp.concatenate([v, jnp.ones(v.shape, v.dtype)], axis=1)


def tile_rows(x, i):
    return x[i * GROUPS * TILE : (i + 1) * GROUPS * TILE]


def edge_mask(above):
    r = lax.broadcasted_iota(jnp.int32, (TILE, TILE), 0)
    c = lax.broadcasted_iota(jnp.int32, (TILE, TILE), 1)
    return jnp.concatenate([c > r if above else c <= r] * GROUPS, axis=0)


def triangle_scores(q2, k_aug, above):
    mask = edge_mask(above)
    seen = [[] for _ in range(TILES)]
    for t in range(TILES):
        first, end = (0, t + 1) if above else (t, TILES)
        rows = q2[first * GROUPS * TILE : end * GROUPS * TILE]
        s = dot_nt(rows, k_aug[t * TILE : (t + 1) * TILE])
        for i in range(first, end):
            part = tile_rows(s, i - first)
            if i == t:
                part = jnp.where(mask, part, HIDDEN)
            seen[i].append(part)
    return seen


def triangle_values(probs, v_aug, above):
    total = [None] * TILES
    for t in range(TILES):
        first, end = (0, t + 1) if above else (t, TILES)
        rows = jnp.concatenate(
            [probs[i][t - i if above else t] for i in range(first, end)], axis=0
        )
        o = dot_nn(rows, v_aug[t * TILE : (t + 1) * TILE])
        for i in range(first, end):
            part = tile_rows(o, i - first)
            total[i] = part if total[i] is None else total[i] + part
    return total


def row_max(parts):
    top = parts[0]
    for part in parts[1:]:
        top = jnp.maximum(top, part)
    return jnp.max(top, axis=-1, keepdims=True)


def weights(parts, m):
    wide = jnp.concatenate([m] * (TILE // HEAD_DIM), axis=1)
    return [jnp.exp2((part - wide) * EXP_SCALE).astype(jnp.bfloat16) for part in parts]


def state_slices(base, g):
    for i in range(TILES):
        for j in range(GROUPS):
            rows = slice(base + i * TILE, base + (i + 1) * TILE)
            yield i, slice(j * TILE, (j + 1) * TILE), rows, head_cols(GROUPS * g + j)


def load_state(ref, base, g):
    parts = [[] for _ in range(TILES)]
    for i, _, rows, cols in state_slices(base, g):
        parts[i].append(ref[rows, cols])
    return [jnp.concatenate(p, axis=0) for p in parts]


def own_kernel(h, q, k, v, hot, acc, mx, ls):
    for role in range(2):
        base = role * HALF
        seen = slice(base, base + HALF)
        for g in range(PAIR):
            own = head_cols(PAIR * h + g)
            q2 = stacked_queries(q, hot, base, (PAIR * h + g) * GROUPS)
            k_aug = jnp.concatenate([k[seen, own], hot[seen, :]], axis=1)
            scores = triangle_scores(q2, k_aug, False)
            tops = [
                jnp.broadcast_to(row_max(parts), (GROUPS * TILE, HEAD_DIM)) for parts in scores
            ]
            probs = [weights(parts, m) for parts, m in zip(scores, tops)]
            o = triangle_values(probs, with_ones(v[seen, own]), False)
            for i, mine, rows, cols in state_slices(base, g):
                acc[rows, cols] = o[i][mine, :HEAD_DIM]
                ls[rows, cols] = o[i][mine, HEAD_DIM:]
                mx[rows, cols] = tops[i][mine]


STATE = jax.ShapeDtypeStruct((2 * HALF, 2 * PAIR * HEAD_DIM), jnp.float32)


def cost(gflop):
    return pl.CostEstimate(
        flops=gflop << 30, bytes_accessed=8 << 20, transcendentals=2 << 20
    )


def own(h, q, k, v, hot):
    return pl.pallas_call(
        functools.partial(own_kernel, h),
        out_shape=(STATE,) * 3,
        in_specs=[VMEM] * 4,
        out_specs=[VMEM] * 3,
        compiler_params=PARAMS,
        cost_estimate=cost(5),
    )(q, k, v, hot)


def far_kernel(h, n, idx, q, hot, zp, za, zb, pa, pb, *rest):
    (acc0, mx0, ls0), (acc, mx, ls) = rest[:3], rest[3:6]
    far, seg, sem, seg_sem = rest[6:]
    from_partner = idx[0] >= n - 2
    id_rows = pl.ds(HALF, 8)

    def fetch(role, src):
        return pltpu.make_async_copy(src, far.at[role], sem.at[role])

    def fetch_ids(role, src):
        return pltpu.make_async_copy(src, seg.at[role], seg_sem.at[role])

    pair = pl.ds(h * SECOND, HALF)
    whole = pl.ds(0, HALF)
    back = (za.at[whole], zb)[h]
    partner = (pa.at[whole], pb)[h]
    fetch_ids(0, zp.at[id_rows]).start()
    fetch(0, zp.at[pair]).start()

    @pl.when(from_partner)
    def _():
        fetch_ids(1, pa.at[id_rows]).start()
        fetch(1, partner).start()

    @pl.when(jnp.logical_not(from_partner))
    def _():
        fetch_ids(1, za.at[id_rows]).start()
        fetch(1, back).start()

    for role in range(2):
        fetch_ids(role, zp.at[id_rows]).wait()
    hots = [one_hot_keys(seg[role, 0:1, :]) for role in range(2)]
    for role in range(2):
        fetch(role, zp.at[pair]).wait()
    for role in range(2):
        base = role * HALF
        for g in range(PAIR):
            q2 = stacked_queries(q, hot, base, (PAIR * h + g) * GROUPS)
            keys = far[role, :, head_cols(g)]
            k_aug = jnp.concatenate([keys, hots[role]], axis=1)
            scores = triangle_scores(q2, k_aug, True)
            old = load_state(mx0, base, g)
            tops = [jnp.maximum(m, row_max(parts)) for m, parts in zip(old, scores)]
            probs = [weights(parts, m) for parts, m in zip(scores, tops)]
            v_aug = with_ones(far[role, :, head_cols(PAIR + g)])
            o = triangle_values(probs, v_aug, True)
            for i, mine, rows, cols in state_slices(base, g):
                keep = jnp.exp2((old[i][mine] - tops[i][mine]) * EXP_SCALE)
                acc[rows, cols] = keep * acc0[rows, cols] + o[i][mine, :HEAD_DIM]
                ls[rows, cols] = keep * ls0[rows, cols] + o[i][mine, HEAD_DIM:]
                mx[rows, cols] = tops[i][mine]


def far(h, n, idx, q, hot, zp, za, zb, pa, pb, state):
    return pl.pallas_call(
        functools.partial(far_kernel, h, n),
        out_shape=(STATE,) * 3,
        in_specs=[SMEM] + [VMEM] * 2 + [ANY] * 5 + [VMEM] * 3,
        out_specs=[VMEM] * 3,
        scratch_shapes=[
            pltpu.VMEM((2, HALF, HALF), jnp.bfloat16),
            pltpu.VMEM((2, 8, HALF), jnp.bfloat16),
            pltpu.SemaphoreType.DMA((2,)),
            pltpu.SemaphoreType.DMA((2,)),
        ],
        compiler_params=PARAMS,
        cost_estimate=cost(5),
    )(idx, q, hot, zp, za, zb, pa, pb, *state)


def finish(h, role, q, hot, piece, hot_mid, state, out, o_buf, out_sem):
    acc, mx, ls = state
    base = role * HALF
    sends = []
    for g in range(PAIR):
        q2 = stacked_queries(q, hot, base, (PAIR * h + g) * GROUPS)
        k_aug = jnp.concatenate([piece[0:HALF, head_cols(g)], hot_mid], axis=1)
        v_aug = with_ones(piece[0:HALF, head_cols(PAIR + g)])
        for t in range(TILES):
            s = dot_nt(tile_rows(q2, t), k_aug)
            old = load_state(mx, base, g)[t]
            m = jnp.maximum(old, jnp.max(s, axis=-1, keepdims=True))
            keep = jnp.exp2((old - m) * EXP_SCALE)
            wide = jnp.concatenate([m] * (HALF // HEAD_DIM), axis=1)
            p = jnp.exp2((s - wide) * EXP_SCALE).astype(jnp.bfloat16)
            o = dot_nn(p, v_aug)
            for i, mine, rows, cols in state_slices(base, g):
                if i != t:
                    continue
                total = keep[mine] * ls[rows, cols] + o[mine, HEAD_DIM:]
                value = keep[mine] * acc[rows, cols] + o[mine, :HEAD_DIM]
                o_buf[rows, cols] = (value * (1.0 / total)).astype(jnp.bfloat16)
        part = pl.ds(g * GROUPS * HEAD_DIM, GROUPS * HEAD_DIM)
        to = pl.ds((PAIR * h + g) * GROUPS * HEAD_DIM, GROUPS * HEAD_DIM)
        here = pl.ds(base, HALF)
        sends.append(
            pltpu.make_async_copy(
                o_buf.at[here, part], out.at[here, to], out_sem.at[PAIR * role + g]
            )
        )
        sends[-1].start()
    return sends


def first_pair_kernel(
    n, idx, q, hot, r1, pa, pb, d1, f1, k, v, *rest
):
    state1, state2 = rest[:3], rest[3:6]
    out, hots, mid, seg, sem, extra, extra_sem, o_buf, out_sem = rest[6:]
    odd = idx[0] % 2 == 1
    end = idx[0] == n - 1
    width = PAIR * HEAD_DIM
    whole, id_rows = pl.ds(0, HALF), pl.ds(HALF, 8)
    cols = [pl.ds(part * width, width) for part in range(2)]

    def fetch(role, ids, srcs):
        pltpu.make_async_copy(ids.at[id_rows], seg.at[role], sem.at[role, 2]).start()
        for i, src in enumerate(srcs):
            pltpu.make_async_copy(src, mid.at[role, :, cols[i]], sem.at[role, i]).start()

    def columns(ref):
        return [ref.at[whole, c] for c in cols]

    def own_front(h):
        return [x.at[whole, pl.ds(h * width, width)] for x in (k, v)]

    def fetch_extra(role, srcs):
        return [
            pltpu.make_async_copy(src, extra.at[role, :, cols[i]], extra_sem.at[role, i])
            for i, src in enumerate(srcs)
        ]

    for role, local, here, sent in ((0, odd, pa, r1), (1, end, None, d1)):

        @pl.when(local)
        def _():
            if role == 0:
                fetch(role, here, columns(here))
                srcs = columns(pb)
            else:
                fetch(role, f1, own_front(0))
                srcs = own_front(1)
            for copy in fetch_extra(role, srcs):
                copy.start()

        @pl.when(jnp.logical_not(local))
        def _():
            fetch(role, sent, columns(sent))

    for role in range(2):
        for i in range(2):
            pltpu.make_async_copy(
                pa.at[whole, cols[i]], mid.at[role, :, cols[i]], sem.at[role, i]
            ).wait()
        pltpu.make_async_copy(pa.at[id_rows], seg.at[role], sem.at[role, 2]).wait()
    sends = []
    for role in range(2):
        hot_mid = one_hot_keys(seg[role, 0:1, :])
        hots[role] = hot_mid
        sends += finish(
            0, role, q, hot, mid.at[role], hot_mid, state1, out, o_buf, out_sem
        )
    for copy in sends:
        copy.wait()

    @pl.when(idx[0] == 0)
    def _():
        acc, _, ls = state2
        o_buf[0:HALF, :] = (acc[0:HALF, :] * (1.0 / ls[0:HALF, :])).astype(jnp.bfloat16)
        second = pl.ds(2 * width, 2 * width)
        copy = pltpu.make_async_copy(
            o_buf.at[whole], out.at[whole, second], out_sem.at[0]
        )
        copy.start()
        copy.wait()

    for role, local in ((0, odd), (1, end)):

        @pl.when(local)
        def _():
            for copy in fetch_extra(role, columns(pb)):
                copy.wait()
            for copy in finish(
                1, role, q, hot, extra.at[role], hots[role], state2, out, o_buf, out_sem
            ):
                copy.wait()


OUT_SCRATCH = (
    pltpu.VMEM((2 * HALF, 2 * PAIR * HEAD_DIM), jnp.bfloat16),
    pltpu.SemaphoreType.DMA((2 * PAIR,)),
)


def first_pair(n, idx, q, hot, pieces, state1, state2):
    piece = pltpu.VMEM((2, HALF, HALF), jnp.bfloat16)
    return pl.pallas_call(
        functools.partial(first_pair_kernel, n),
        out_shape=(
            jax.ShapeDtypeStruct(q.shape, q.dtype),
            jax.ShapeDtypeStruct((2, HALF, HEAD_DIM), jnp.bfloat16),
        ),
        in_specs=[SMEM] + [VMEM] * 2 + [ANY] * len(pieces) + [VMEM] * 6,
        out_specs=(ANY, VMEM),
        scratch_shapes=[
            piece,
            pltpu.VMEM((2, 8, HALF), jnp.bfloat16),
            pltpu.SemaphoreType.DMA((2, 3)),
            piece,
            pltpu.SemaphoreType.DMA((2, 2)),
            *OUT_SCRATCH,
        ],
        compiler_params=PARAMS,
        cost_estimate=cost(5),
        name="last0",
    )(idx, q, hot, *pieces, *state1, *state2)


def second_pair_kernel(role, n, idx, q, hot, piece, hots, acc, mx, ls, _, out, o_buf, out_sem):
    if role == 0:
        needed = (idx[0] % 2 == 0) & (idx[0] > 0)
    else:
        needed = idx[0] < n - 1

    @pl.when(needed)
    def _():
        state = (acc, mx, ls)
        for copy in finish(
            1, role, q, hot, piece, hots[role], state, out, o_buf, out_sem
        ):
            copy.wait()


def second_pair(role, n, idx, q, hot, piece, hots, state, out):
    return pl.pallas_call(
        functools.partial(second_pair_kernel, role, n),
        out_shape=jax.ShapeDtypeStruct(q.shape, q.dtype),
        in_specs=[SMEM] + [VMEM] * 7 + [ANY],
        out_specs=ANY,
        input_output_aliases={8: 0},
        scratch_shapes=OUT_SCRATCH,
        compiler_params=PARAMS,
        cost_estimate=cost(5),
    )(idx, q, hot, piece, hots, *state, out)


def body(queries, key_states, value_states, segment_ids):
    n = lax.axis_size("seq")
    seq = lax.axis_index("seq").astype(jnp.int32)
    idx = seq.reshape(1)
    lane = jnp.arange(HEAD_DIM, dtype=jnp.int32)
    hot = (segment_ids[:, None] + 1 == lane[None, :]).astype(jnp.bfloat16)

    partner = [(i, i ^ 1) for i in range(n)]
    up_two = [(i, i + 2) for i in range(n - 2)]
    down_two = [(i + 2, i) for i in range(n - 2)]
    relay = [(i, i + 2) for i in range(0, n - 2, 2)]

    def send(x, route):
        return lax.ppermute(x, "seq", route)

    q, k, v = queries, key_states, value_states
    in_hbm = tuple(
        pltpu.with_memory_space_constraint(x, pltpu.HBM)
        for x in (k, v, segment_ids.reshape(1, 2 * HALF))
    )
    f1, front = pack_front(*in_hbm)
    pa = send(f1, partner)
    zp = send(front, up_two)
    b1, f2, b2 = pack_rest(*in_hbm)
    za = send(b1, down_two)
    pb = send(f2, partner)
    zb = send(b2, down_two)
    state1 = own(0, q, k, v, hot)
    r1 = send(pa, relay)
    state2 = own(1, q, k, v, hot)
    even = seq % 2 == 0
    back = jnp.where(even, za, b1)
    d1 = send(back, partner)
    r2 = send(pb, relay)
    state1 = far(0, n, idx, q, hot, zp, za, za, pa, pa, state1)
    back = jnp.where(even, zb, b2)
    d2 = send(back, partner)
    state2 = far(1, n, idx, q, hot, zp, za, zb, pa, pb, state2)

    pieces = (r1, pa, pb, d1, f1, k, v)
    out, hots = first_pair(n, idx, q, hot, pieces, state1, state2)
    out = second_pair(1, n, idx, q, hot, d2, hots, state2, out)
    return second_pair(0, n, idx, q, hot, r2, hots, state2, out)


def solution(mesh):
    in_specs = (
        P(("grp", "seq"), "head"),
        P(("grp", "seq"), "head"),
        P(("grp", "seq"), "head"),
        P(("grp", "seq")),
    )
    out_specs = P(("grp", "seq"), "head")
    return jax.shard_map(body, mesh=mesh, in_specs=in_specs, out_specs=out_specs, check_vma=False)
```

```python
import functools
import math

import jax
import jax.numpy as jnp
from jax import lax
from jax.experimental import pallas as pl
from jax.experimental.pallas import tpu as pltpu
from jax.sharding import PartitionSpec as P

HEAD_DIM = 128
GROUPS = 2
HALF = 512
PAIR = 2
TILE = 256
TILES = HALF // TILE

EXP_SCALE = 168.0 ** (-0.5) * math.log2(math.e)
HIDDEN = -1e30
MATCH = 12288.0

VMEM = pl.BlockSpec(memory_space=pltpu.VMEM)
SMEM = pl.BlockSpec(memory_space=pltpu.SMEM)
ANY = pl.BlockSpec(memory_space=pl.ANY)
HBM = pl.BlockSpec(memory_space=pltpu.HBM)
PARAMS = pltpu.CompilerParams(vmem_limit_bytes=10 << 20)


def dot_nt(a, b):
    return lax.dot_general(
        a, b, (((1,), (1,)), ((), ())), preferred_element_type=jnp.float32
    )


def dot_nn(a, b):
    return lax.dot_general(
        a, b, (((1,), (0,)), ((), ())), preferred_element_type=jnp.float32
    )


def head_cols(head):
    return slice(head * HEAD_DIM, (head + 1) * HEAD_DIM)


SECOND = HALF + 16
FRONT = SECOND + HALF


def ids_row(ids_v, role):
    row = ids_v[:, role * HALF : (role + 1) * HALF].astype(jnp.float32) + 1.0
    return jnp.broadcast_to(row, (16, HALF)).astype(jnp.bfloat16)


def block_copies(k, v, role, h, target, sem):
    rows = pl.ds(role * HALF, HALF)
    cols = pl.ds(h * PAIR * HEAD_DIM, PAIR * HEAD_DIM)
    return [
        pltpu.make_async_copy(
            src.at[rows, cols],
            target.at[:, pl.ds(part * PAIR * HEAD_DIM, PAIR * HEAD_DIM)],
            sem.at[part],
        )
        for part, src in enumerate((k, v))
    ]


def pack_front_kernel(k, v, ids, f1, front, ids_v, stage, sem, ids_sem, out_sem):
    get_ids = pltpu.make_async_copy(ids, ids_v, ids_sem)
    get_ids.start()
    parts = (pl.ds(0, SECOND), pl.ds(SECOND, HALF))
    copies = [
        block_copies(k, v, 0, h, stage.at[pl.ds(h * SECOND, HALF)], sem.at[h]) for h in range(2)
    ]
    for copy in copies[0] + copies[1]:
        copy.start()
    get_ids.wait()
    stage[HALF:SECOND, :] = ids_row(ids_v, 0)
    first = pl.ds(0, HALF + 8)
    sends = [
        pltpu.make_async_copy(stage.at[first], f1, out_sem.at[0]),
        pltpu.make_async_copy(stage.at[parts[0]], front.at[parts[0]], out_sem.at[1]),
        pltpu.make_async_copy(stage.at[parts[1]], front.at[parts[1]], out_sem.at[2]),
    ]
    for h in range(2):
        for copy in copies[h]:
            copy.wait()
        for send in sends[2 * h : 2 + h]:
            send.start()
    for send in sends:
        send.wait()


def pack_front(k, v, ids):
    return pl.pallas_call(
        pack_front_kernel,
        out_shape=tuple(
            jax.ShapeDtypeStruct((r, HALF), jnp.bfloat16) for r in (HALF + 8, FRONT)
        ),
        in_specs=[HBM] * 3,
        out_specs=[HBM] * 2,
        scratch_shapes=[
            pltpu.VMEM((1, 2 * HALF), jnp.int32),
            pltpu.VMEM((FRONT, HALF), jnp.bfloat16),
            pltpu.SemaphoreType.DMA((2, 2)),
            pltpu.SemaphoreType.DMA,
            pltpu.SemaphoreType.DMA((3,)),
        ],
        compiler_params=PARAMS,
        cost_estimate=pl.CostEstimate(
            flops=1 << 20, bytes_accessed=2 << 20, transcendentals=0
        ),
        name="pack0",
    )(k, v, ids)


def head_copies(k, v, head, target, sem):
    return [
        pltpu.make_async_copy(
            src.at[pl.ds(0, HALF), pl.ds(head * HEAD_DIM, HEAD_DIM)],
            target.at[:, pl.ds(part * HEAD_DIM, HEAD_DIM)],
            sem.at[part],
        )
        for part, src in enumerate((k, v))
    ]


def pack_rest_kernel(k, v, ids, b1, f2, f3, b2, ids_v, stage, sem, ids_sem, out_sem):
    get_ids = pltpu.make_async_copy(ids, ids_v, ids_sem)
    get_ids.start()
    whole = pl.ds(0, HALF)
    areas = [
        stage.at[0, pl.ds(0, HALF + 8)],
        stage.at[1, whole, pl.ds(0, 2 * HEAD_DIM)],
        stage.at[2, whole, pl.ds(0, 2 * HEAD_DIM)],
        stage.at[3, whole],
    ]
    copies = [
        block_copies(k, v, 1, 0, stage.at[0, whole], sem.at[0]),
        head_copies(k, v, PAIR, areas[1], sem.at[1]),
        head_copies(k, v, PAIR + 1, areas[2], sem.at[2]),
        block_copies(k, v, 1, 1, areas[3], sem.at[3]),
    ]
    for pair in copies:
        for copy in pair:
            copy.start()
    get_ids.wait()
    stage[0, HALF:SECOND, :] = ids_row(ids_v, 1)
    sends = []
    for i, piece in enumerate((b1, f2, f3, b2)):
        for copy in copies[i]:
            copy.wait()
        sends.append(pltpu.make_async_copy(areas[i], piece, out_sem.at[i]))
        sends[-1].start()
    for send in sends:
        send.wait()


def pack_rest(k, v, ids):
    shapes = (
        (HALF + 8, HALF),
        (HALF, 2 * HEAD_DIM),
        (HALF, 2 * HEAD_DIM),
        (HALF, HALF),
    )
    return pl.pallas_call(
        pack_rest_kernel,
        out_shape=tuple(jax.ShapeDtypeStruct(x, jnp.bfloat16) for x in shapes),
        in_specs=[HBM] * 3,
        out_specs=[HBM] * 4,
        scratch_shapes=[
            pltpu.VMEM((1, 2 * HALF), jnp.int32),
            pltpu.VMEM((4, SECOND, HALF), jnp.bfloat16),
            pltpu.SemaphoreType.DMA((4, 2)),
            pltpu.SemaphoreType.DMA,
            pltpu.SemaphoreType.DMA((4,)),
        ],
        compiler_params=PARAMS,
        cost_estimate=pl.CostEstimate(
            flops=1 << 20, bytes_accessed=3 << 20, transcendentals=0
        ),
        name="pack1",
    )(k, v, ids)


def one_hot_keys(row):
    lane = lax.broadcasted_iota(jnp.int32, (HEAD_DIM, HALF), 0).astype(jnp.float32)
    hot = jnp.where(lane == row.astype(jnp.float32), 1.0, 0.0)
    return hot.T.astype(jnp.bfloat16)


def stacked_queries(q, hot, base, first_head):
    blocks = []
    for i in range(TILES):
        rows = slice(base + i * TILE, base + (i + 1) * TILE)
        mark = hot[rows, :] * jnp.bfloat16(MATCH)
        for j in range(GROUPS):
            blocks.append(jnp.concatenate([q[rows, head_cols(first_head + j)], mark], axis=1))
    return jnp.concatenate(blocks, axis=0)


def with_ones(v):
    return jnp.concatenate([v, jnp.ones(v.shape, v.dtype)], axis=1)


def tile_rows(x, i):
    return x[i * GROUPS * TILE : (i + 1) * GROUPS * TILE]


def edge_mask(above):
    r = lax.broadcasted_iota(jnp.int32, (TILE, TILE), 0)
    c = lax.broadcasted_iota(jnp.int32, (TILE, TILE), 1)
    return jnp.concatenate([c > r if above else c <= r] * GROUPS, axis=0)


def triangle_scores(q2, k_aug, above):
    mask = edge_mask(above)
    seen = [[] for _ in range(TILES)]
    for t in range(TILES):
        first, end = (0, t + 1) if above else (t, TILES)
        rows = q2[first * GROUPS * TILE : end * GROUPS * TILE]
        s = dot_nt(rows, k_aug[t * TILE : (t + 1) * TILE])
        for i in range(first, end):
            part = tile_rows(s, i - first)
            if i == t:
                part = jnp.where(mask, part, HIDDEN)
            seen[i].append(part)
    return seen


def triangle_values(probs, v_aug, above):
    total = [None] * TILES
    for t in range(TILES):
        first, end = (0, t + 1) if above else (t, TILES)
        rows = jnp.concatenate(
            [probs[i][t - i if above else t] for i in range(first, end)], axis=0
        )
        o = dot_nn(rows, v_aug[t * TILE : (t + 1) * TILE])
        for i in range(first, end):
            part = tile_rows(o, i - first)
            total[i] = part if total[i] is None else total[i] + part
    return total


def row_max(parts):
    top = parts[0]
    for part in parts[1:]:
        top = jnp.maximum(top, part)
    return jnp.max(top, axis=-1, keepdims=True)


def weights(parts, m):
    wide = jnp.concatenate([m] * (TILE // HEAD_DIM), axis=1)
    return [jnp.exp2((part - wide) * EXP_SCALE).astype(jnp.bfloat16) for part in parts]


def state_slices(base, g):
    for i in range(TILES):
        for j in range(GROUPS):
            rows = slice(base + i * TILE, base + (i + 1) * TILE)
            yield i, slice(j * TILE, (j + 1) * TILE), rows, head_cols(GROUPS * g + j)


def load_state(ref, base, g):
    parts = [[] for _ in range(TILES)]
    for i, _, rows, cols in state_slices(base, g):
        parts[i].append(ref[rows, cols])
    return [jnp.concatenate(p, axis=0) for p in parts]


def own_kernel(h, q, k, v, hot, acc, mx, ls):
    for role in range(2):
        base = role * HALF
        seen = slice(base, base + HALF)
        for g in range(PAIR):
            own = head_cols(PAIR * h + g)
            q2 = stacked_queries(q, hot, base, (PAIR * h + g) * GROUPS)
            k_aug = jnp.concatenate([k[seen, own], hot[seen, :]], axis=1)
            scores = triangle_scores(q2, k_aug, False)
            tops = [
                jnp.broadcast_to(row_max(parts), (GROUPS * TILE, HEAD_DIM)) for parts in scores
            ]
            probs = [weights(parts, m) for parts, m in zip(scores, tops)]
            o = triangle_values(probs, with_ones(v[seen, own]), False)
            for i, mine, rows, cols in state_slices(base, g):
                acc[rows, cols] = o[i][mine, :HEAD_DIM]
                ls[rows, cols] = o[i][mine, HEAD_DIM:]
                mx[rows, cols] = tops[i][mine]


STATE = jax.ShapeDtypeStruct((2 * HALF, 2 * PAIR * HEAD_DIM), jnp.float32)


def cost(gflop):
    return pl.CostEstimate(
        flops=gflop << 30, bytes_accessed=8 << 20, transcendentals=2 << 20
    )


def own(h, q, k, v, hot):
    return pl.pallas_call(
        functools.partial(own_kernel, h),
        out_shape=(STATE,) * 3,
        in_specs=[VMEM] * 4,
        out_specs=[VMEM] * 3,
        compiler_params=PARAMS,
        cost_estimate=cost(5),
    )(q, k, v, hot)


def by_head(first, second):
    return [
        x.at[:, pl.ds(part * HEAD_DIM, HEAD_DIM)] for part in range(2) for x in (first, second)
    ]


def far_kernel(h, n, idx, q, hot, zp, za, zb, pa, pb2, pb3, *rest):
    (acc0, mx0, ls0), (acc, mx, ls) = rest[:3], rest[3:6]
    far, seg, sem, seg_sem = rest[6:]
    from_partner = idx[0] >= n - 2
    id_rows = pl.ds(HALF, 8)

    def fetch(role, src):
        return pltpu.make_async_copy(src, far.at[role], sem.at[role])

    def fetch_ids(role, src):
        return pltpu.make_async_copy(src, seg.at[role], seg_sem.at[role])

    pair = pl.ds(h * SECOND, HALF)
    whole = pl.ds(0, HALF)
    back = (za.at[whole], zb)[h]
    fetch_ids(0, zp.at[id_rows]).start()
    fetch(0, zp.at[pair]).start()

    @pl.when(from_partner)
    def _():
        fetch_ids(1, pa.at[id_rows]).start()
        if h == 0:
            fetch(1, pa.at[whole]).start()
        else:
            for j, src in enumerate(by_head(pb2, pb3)):
                to = far.at[1, :, pl.ds(j * HEAD_DIM, HEAD_DIM)]
                pltpu.make_async_copy(src, to, sem.at[1]).start()

    @pl.when(jnp.logical_not(from_partner))
    def _():
        fetch_ids(1, za.at[id_rows]).start()
        fetch(1, back).start()

    for role in range(2):
        fetch_ids(role, zp.at[id_rows]).wait()
    hots = [one_hot_keys(seg[role, 0:1, :]) for role in range(2)]
    for role in range(2):
        fetch(role, zp.at[pair]).wait()
    for role in range(2):
        base = role * HALF
        for g in range(PAIR):
            q2 = stacked_queries(q, hot, base, (PAIR * h + g) * GROUPS)
            keys = far[role, :, head_cols(g)]
            k_aug = jnp.concatenate([keys, hots[role]], axis=1)
            scores = triangle_scores(q2, k_aug, True)
            old = load_state(mx0, base, g)
            tops = [jnp.maximum(m, row_max(parts)) for m, parts in zip(old, scores)]
            probs = [weights(parts, m) for parts, m in zip(scores, tops)]
            v_aug = with_ones(far[role, :, head_cols(PAIR + g)])
            o = triangle_values(probs, v_aug, True)
            for i, mine, rows, cols in state_slices(base, g):
                keep = jnp.exp2((old[i][mine] - tops[i][mine]) * EXP_SCALE)
                acc[rows, cols] = keep * acc0[rows, cols] + o[i][mine, :HEAD_DIM]
                ls[rows, cols] = keep * ls0[rows, cols] + o[i][mine, HEAD_DIM:]
                mx[rows, cols] = tops[i][mine]


def far(h, n, idx, q, hot, zp, za, zb, pa, pb2, pb3, state):
    return pl.pallas_call(
        functools.partial(far_kernel, h, n),
        out_shape=(STATE,) * 3,
        in_specs=[SMEM] + [VMEM] * 2 + [ANY] * 6 + [VMEM] * 3,
        out_specs=[VMEM] * 3,
        scratch_shapes=[
            pltpu.VMEM((2, HALF, HALF), jnp.bfloat16),
            pltpu.VMEM((2, 8, HALF), jnp.bfloat16),
            pltpu.SemaphoreType.DMA((2,)),
            pltpu.SemaphoreType.DMA((2,)),
        ],
        compiler_params=PARAMS,
        cost_estimate=cost(5),
    )(idx, q, hot, zp, za, zb, pa, pb2, pb3, *state)


BOTH = ((0, 0, PAIR), (1, 1, PAIR + 1))


def finish(h, role, q, hot, piece, hot_mid, state, out, o_buf, out_sem, heads=BOTH):
    acc, mx, ls = state
    base = role * HALF
    sends = []
    for g, k_at, v_at in heads:
        q2 = stacked_queries(q, hot, base, (PAIR * h + g) * GROUPS)
        k_aug = jnp.concatenate([piece[0:HALF, head_cols(k_at)], hot_mid], axis=1)
        v_aug = with_ones(piece[0:HALF, head_cols(v_at)])
        for t in range(TILES):
            s = dot_nt(tile_rows(q2, t), k_aug)
            old = load_state(mx, base, g)[t]
            m = jnp.maximum(old, jnp.max(s, axis=-1, keepdims=True))
            keep = jnp.exp2((old - m) * EXP_SCALE)
            wide = jnp.concatenate([m] * (HALF // HEAD_DIM), axis=1)
            p = jnp.exp2((s - wide) * EXP_SCALE).astype(jnp.bfloat16)
            o = dot_nn(p, v_aug)
            for i, mine, rows, cols in state_slices(base, g):
                if i != t:
                    continue
                total = keep[mine] * ls[rows, cols] + o[mine, HEAD_DIM:]
                value = keep[mine] * acc[rows, cols] + o[mine, :HEAD_DIM]
                o_buf[rows, cols] = (value * (1.0 / total)).astype(jnp.bfloat16)
        part = pl.ds(g * GROUPS * HEAD_DIM, GROUPS * HEAD_DIM)
        to = pl.ds((PAIR * h + g) * GROUPS * HEAD_DIM, GROUPS * HEAD_DIM)
        here = pl.ds(base, HALF)
        sends.append(
            pltpu.make_async_copy(
                o_buf.at[here, part], out.at[here, to], out_sem.at[PAIR * role + g]
            )
        )
        sends[-1].start()
    return sends


def first_pair_kernel(
    n, idx, q, hot, r1, pa, pb2, pb3, d1, f1, k, v, *rest
):
    state1, state2 = rest[:3], rest[3:6]
    out, hots, mid, seg, sem, extra, extra_sem, o_buf, out_sem = rest[6:]
    odd = idx[0] % 2 == 1
    end = idx[0] == n - 1
    width = PAIR * HEAD_DIM
    whole, id_rows = pl.ds(0, HALF), pl.ds(HALF, 8)
    cols = [pl.ds(part * width, width) for part in range(2)]

    def fetch(role, ids, srcs):
        pltpu.make_async_copy(ids.at[id_rows], seg.at[role], sem.at[role, 2]).start()
        for i, src in enumerate(srcs):
            pltpu.make_async_copy(src, mid.at[role, :, cols[i]], sem.at[role, i]).start()

    def columns(ref):
        return [ref.at[whole, c] for c in cols]

    def own_front(h):
        return [x.at[whole, pl.ds(h * width, width)] for x in (k, v)]

    def fetch_extra(role, srcs):
        return [
            pltpu.make_async_copy(
                src,
                extra.at[role, :, pl.ds(i * HEAD_DIM, HEAD_DIM)],
                extra_sem.at[role, i],
            )
            for i, src in enumerate(srcs)
        ]

    for role, local, here, sent in ((0, odd, pa, r1), (1, end, None, d1)):

        @pl.when(local)
        def _():
            if role == 0:
                fetch(role, here, columns(here))
                srcs = by_head(pb2, pb3)
            else:
                fetch(role, f1, own_front(0))
                srcs = [
                    x.at[whole, pl.ds(head * HEAD_DIM, HEAD_DIM)]
                    for x in (k, v)
                    for head in (PAIR, PAIR + 1)
                ]
            for copy in fetch_extra(role, srcs):
                copy.start()

        @pl.when(jnp.logical_not(local))
        def _():
            fetch(role, sent, columns(sent))

    for role in range(2):
        for i in range(2):
            pltpu.make_async_copy(
                pa.at[whole, cols[i]], mid.at[role, :, cols[i]], sem.at[role, i]
            ).wait()
        pltpu.make_async_copy(pa.at[id_rows], seg.at[role], sem.at[role, 2]).wait()
    sends = []
    for role in range(2):
        hot_mid = one_hot_keys(seg[role, 0:1, :])
        hots[role] = hot_mid
        sends += finish(
            0, role, q, hot, mid.at[role], hot_mid, state1, out, o_buf, out_sem
        )
    for copy in sends:
        copy.wait()

    @pl.when(idx[0] == 0)
    def _():
        acc, _, ls = state2
        o_buf[0:HALF, :] = (acc[0:HALF, :] * (1.0 / ls[0:HALF, :])).astype(jnp.bfloat16)
        second = pl.ds(2 * width, 2 * width)
        copy = pltpu.make_async_copy(
            o_buf.at[whole], out.at[whole, second], out_sem.at[0]
        )
        copy.start()
        copy.wait()

    for role, local in ((0, odd), (1, end)):

        @pl.when(local)
        def _():
            for copy in fetch_extra(role, by_head(pb2, pb3)):
                copy.wait()
            for copy in finish(
                1, role, q, hot, extra.at[role], hots[role], state2, out, o_buf, out_sem
            ):
                copy.wait()


OUT_SCRATCH = (
    pltpu.VMEM((2 * HALF, 2 * PAIR * HEAD_DIM), jnp.bfloat16),
    pltpu.SemaphoreType.DMA((2 * PAIR,)),
)


def first_pair(n, idx, q, hot, pieces, state1, state2):
    piece = pltpu.VMEM((2, HALF, HALF), jnp.bfloat16)
    return pl.pallas_call(
        functools.partial(first_pair_kernel, n),
        out_shape=(
            jax.ShapeDtypeStruct(q.shape, q.dtype),
            jax.ShapeDtypeStruct((2, HALF, HEAD_DIM), jnp.bfloat16),
        ),
        in_specs=[SMEM] + [VMEM] * 2 + [ANY] * len(pieces) + [VMEM] * 6,
        out_specs=(ANY, VMEM),
        scratch_shapes=[
            piece,
            pltpu.VMEM((2, 8, HALF), jnp.bfloat16),
            pltpu.SemaphoreType.DMA((2, 3)),
            piece,
            pltpu.SemaphoreType.DMA((2, 4)),
            *OUT_SCRATCH,
        ],
        compiler_params=PARAMS,
        cost_estimate=cost(5),
        name="last0",
    )(idx, q, hot, *pieces, *state1, *state2)


ALONE = (((0, 0, 1),), ((1, 0, 1),))


def second_pair_kernel(n, idx, q, hot, *rest):
    *pieces, hots, acc, mx, ls, _, out, o_buf, out_sem = rest
    relayed = (idx[0] % 2 == 0) & (idx[0] > 0)

    def go(jobs):
        copies = []
        for role, piece, heads in jobs:
            copies += finish(
                1, role, q, hot, piece, hots[role], (acc, mx, ls), out, o_buf, out_sem, heads
            )
        for copy in copies:
            copy.wait()

    if len(pieces) == 1:

        @pl.when(relayed)
        def _():
            go([(0, pieces[0], ALONE[1])])

    else:
        front, back = pieces

        @pl.when(relayed)
        def _():
            go([(1, back, BOTH), (0, front, ALONE[0])])

        @pl.when(jnp.logical_not(relayed) & (idx[0] < n - 1))
        def _():
            go([(1, back, BOTH)])


def second_pair(n, idx, q, hot, pieces, hots, state, out):
    count = len(pieces)
    return pl.pallas_call(
        functools.partial(second_pair_kernel, n),
        out_shape=jax.ShapeDtypeStruct(q.shape, q.dtype),
        in_specs=[SMEM] + [VMEM] * (count + 6) + [ANY],
        out_specs=ANY,
        input_output_aliases={count + 7: 0},
        scratch_shapes=OUT_SCRATCH,
        compiler_params=PARAMS,
        cost_estimate=cost(5),
    )(idx, q, hot, *pieces, hots, *state, out)


def body(queries, key_states, value_states, segment_ids):
    n = lax.axis_size("seq")
    seq = lax.axis_index("seq").astype(jnp.int32)
    idx = seq.reshape(1)
    lane = jnp.arange(HEAD_DIM, dtype=jnp.int32)
    hot = (segment_ids[:, None] + 1 == lane[None, :]).astype(jnp.bfloat16)

    partner = [(i, i ^ 1) for i in range(n)]
    up_two = [(i, i + 2) for i in range(n - 2)]
    down_two = [(i + 2, i) for i in range(n - 2)]
    relay = [(i, i + 2) for i in range(0, n - 2, 2)]

    def send(x, route):
        return lax.ppermute(x, "seq", route)

    q, k, v = queries, key_states, value_states
    in_hbm = tuple(
        pltpu.with_memory_space_constraint(x, pltpu.HBM)
        for x in (k, v, segment_ids.reshape(1, 2 * HALF))
    )
    f1, front = pack_front(*in_hbm)
    pa = send(f1, partner)
    zp = send(front, up_two)
    b1, f2, f3, b2 = pack_rest(*in_hbm)
    za = send(b1, down_two)
    pb2 = send(f2, partner)
    pb3 = send(f3, partner)
    zb = send(b2, down_two)
    state1 = own(0, q, k, v, hot)
    r1 = send(pa, relay)
    state2 = own(1, q, k, v, hot)
    even = seq % 2 == 0
    back = jnp.where(even, za, b1)
    d1 = send(back, partner)
    r2 = send(pb2, relay)
    state1 = far(0, n, idx, q, hot, zp, za, za, pa, pa, pa, state1)
    back = jnp.where(even, zb, b2)
    d2 = send(back, partner)
    state2 = far(1, n, idx, q, hot, zp, za, zb, pa, pb2, pb3, state2)

    r3 = send(pb3, relay)
    pieces = (r1, pa, pb2, pb3, d1, f1, k, v)
    out, hots = first_pair(n, idx, q, hot, pieces, state1, state2)
    out = second_pair(n, idx, q, hot, (r2, d2), hots, state2, out)
    return second_pair(n, idx, q, hot, (r3,), hots, state2, out)


def solution(mesh):
    in_specs = (
        P(("grp", "seq"), "head"),
        P(("grp", "seq"), "head"),
        P(("grp", "seq"), "head"),
        P(("grp", "seq")),
    )
    out_specs = P(("grp", "seq"), "head")
    return jax.shard_map(body, mesh=mesh, in_specs=in_specs, out_specs=out_specs, check_vma=False)
```

```python
import functools
import math

import jax
import jax.numpy as jnp
from jax import lax
from jax.experimental import pallas as pl
from jax.experimental.pallas import tpu as pltpu
from jax.sharding import PartitionSpec as P

HEAD_DIM = 128
GROUPS = 2
HALF = 512
PAIR = 2
TILE = 256
TILES = HALF // TILE

EXP_SCALE = 168.0 ** (-0.5) * math.log2(math.e)
HIDDEN = -1e30
MATCH = 12288.0

VMEM = pl.BlockSpec(memory_space=pltpu.VMEM)
SMEM = pl.BlockSpec(memory_space=pltpu.SMEM)
ANY = pl.BlockSpec(memory_space=pl.ANY)
HBM = pl.BlockSpec(memory_space=pltpu.HBM)
PARAMS = pltpu.CompilerParams(vmem_limit_bytes=10 << 20)


def dot_nt(a, b):
    return lax.dot_general(
        a, b, (((1,), (1,)), ((), ())), preferred_element_type=jnp.float32
    )


def dot_nn(a, b):
    return lax.dot_general(
        a, b, (((1,), (0,)), ((), ())), preferred_element_type=jnp.float32
    )


def head_cols(head):
    return slice(head * HEAD_DIM, (head + 1) * HEAD_DIM)


SECOND = HALF + 16
FRONT = SECOND + HALF


def ids_row(ids_v, role):
    row = ids_v[:, role * HALF : (role + 1) * HALF].astype(jnp.float32) + 1.0
    return jnp.broadcast_to(row, (16, HALF)).astype(jnp.bfloat16)


def block_copies(k, v, role, h, target, sem):
    rows = pl.ds(role * HALF, HALF)
    cols = pl.ds(h * PAIR * HEAD_DIM, PAIR * HEAD_DIM)
    return [
        pltpu.make_async_copy(
            src.at[rows, cols],
            target.at[:, pl.ds(part * PAIR * HEAD_DIM, PAIR * HEAD_DIM)],
            sem.at[part],
        )
        for part, src in enumerate((k, v))
    ]


def pack_front_kernel(k, v, ids, f1, front, ids_v, stage, sem, ids_sem, out_sem):
    get_ids = pltpu.make_async_copy(ids, ids_v, ids_sem)
    get_ids.start()
    parts = (pl.ds(0, SECOND), pl.ds(SECOND, HALF))
    copies = [
        block_copies(k, v, 0, h, stage.at[pl.ds(h * SECOND, HALF)], sem.at[h]) for h in range(2)
    ]
    for copy in copies[0] + copies[1]:
        copy.start()
    get_ids.wait()
    stage[HALF:SECOND, :] = ids_row(ids_v, 0)
    first = pl.ds(0, HALF + 8)
    sends = [
        pltpu.make_async_copy(stage.at[first], f1, out_sem.at[0]),
        pltpu.make_async_copy(stage.at[parts[0]], front.at[parts[0]], out_sem.at[1]),
        pltpu.make_async_copy(stage.at[parts[1]], front.at[parts[1]], out_sem.at[2]),
    ]
    for h in range(2):
        for copy in copies[h]:
            copy.wait()
        for send in sends[2 * h : 2 + h]:
            send.start()
    for send in sends:
        send.wait()


def pack_front(k, v, ids):
    return pl.pallas_call(
        pack_front_kernel,
        out_shape=tuple(
            jax.ShapeDtypeStruct((r, HALF), jnp.bfloat16) for r in (HALF + 8, FRONT)
        ),
        in_specs=[HBM] * 3,
        out_specs=[HBM] * 2,
        scratch_shapes=[
            pltpu.VMEM((1, 2 * HALF), jnp.int32),
            pltpu.VMEM((FRONT, HALF), jnp.bfloat16),
            pltpu.SemaphoreType.DMA((2, 2)),
            pltpu.SemaphoreType.DMA,
            pltpu.SemaphoreType.DMA((3,)),
        ],
        compiler_params=PARAMS,
        cost_estimate=pl.CostEstimate(
            flops=1 << 20, bytes_accessed=2 << 20, transcendentals=0
        ),
        name="pack0",
    )(k, v, ids)


def head_copies(k, v, head, target, sem):
    return [
        pltpu.make_async_copy(
            src.at[pl.ds(0, HALF), pl.ds(head * HEAD_DIM, HEAD_DIM)],
            target.at[:, pl.ds(part * HEAD_DIM, HEAD_DIM)],
            sem.at[part],
        )
        for part, src in enumerate((k, v))
    ]


def pack_rest_kernel(k, v, ids, b1, f2, f3, b2, ids_v, stage, sem, ids_sem, out_sem):
    get_ids = pltpu.make_async_copy(ids, ids_v, ids_sem)
    get_ids.start()
    whole = pl.ds(0, HALF)
    areas = [
        stage.at[0, pl.ds(0, HALF + 8)],
        stage.at[1, whole, pl.ds(0, 2 * HEAD_DIM)],
        stage.at[2, whole, pl.ds(0, 2 * HEAD_DIM)],
        stage.at[3, whole],
    ]
    copies = [
        block_copies(k, v, 1, 0, stage.at[0, whole], sem.at[0]),
        head_copies(k, v, PAIR, areas[1], sem.at[1]),
        head_copies(k, v, PAIR + 1, areas[2], sem.at[2]),
        block_copies(k, v, 1, 1, areas[3], sem.at[3]),
    ]
    for pair in copies:
        for copy in pair:
            copy.start()
    get_ids.wait()
    stage[0, HALF:SECOND, :] = ids_row(ids_v, 1)
    sends = []
    for i, piece in enumerate((b1, f2, f3, b2)):
        for copy in copies[i]:
            copy.wait()
        sends.append(pltpu.make_async_copy(areas[i], piece, out_sem.at[i]))
        sends[-1].start()
    for send in sends:
        send.wait()


def pack_rest(k, v, ids):
    shapes = (
        (HALF + 8, HALF),
        (HALF, 2 * HEAD_DIM),
        (HALF, 2 * HEAD_DIM),
        (HALF, HALF),
    )
    return pl.pallas_call(
        pack_rest_kernel,
        out_shape=tuple(jax.ShapeDtypeStruct(x, jnp.bfloat16) for x in shapes),
        in_specs=[HBM] * 3,
        out_specs=[HBM] * 4,
        scratch_shapes=[
            pltpu.VMEM((1, 2 * HALF), jnp.int32),
            pltpu.VMEM((4, SECOND, HALF), jnp.bfloat16),
            pltpu.SemaphoreType.DMA((4, 2)),
            pltpu.SemaphoreType.DMA,
            pltpu.SemaphoreType.DMA((4,)),
        ],
        compiler_params=PARAMS,
        cost_estimate=pl.CostEstimate(
            flops=1 << 20, bytes_accessed=3 << 20, transcendentals=0
        ),
        name="pack1",
    )(k, v, ids)


def one_hot_keys(row):
    lane = lax.broadcasted_iota(jnp.int32, (HEAD_DIM, HALF), 0).astype(jnp.float32)
    hot = jnp.where(lane == row.astype(jnp.float32), 1.0, 0.0)
    return hot.T.astype(jnp.bfloat16)


def stacked_queries(q, hot, base, first_head):
    blocks = []
    for i in range(TILES):
        rows = slice(base + i * TILE, base + (i + 1) * TILE)
        mark = hot[rows, :] * jnp.bfloat16(MATCH)
        for j in range(GROUPS):
            blocks.append(jnp.concatenate([q[rows, head_cols(first_head + j)], mark], axis=1))
    return jnp.concatenate(blocks, axis=0)


def with_ones(v):
    return jnp.concatenate([v, jnp.ones(v.shape, v.dtype)], axis=1)


def tile_rows(x, i):
    return x[i * GROUPS * TILE : (i + 1) * GROUPS * TILE]


def edge_mask(above):
    r = lax.broadcasted_iota(jnp.int32, (TILE, TILE), 0)
    c = lax.broadcasted_iota(jnp.int32, (TILE, TILE), 1)
    return jnp.concatenate([c > r if above else c <= r] * GROUPS, axis=0)


def triangle_scores(q2, k_aug, above):
    mask = edge_mask(above)
    seen = [[] for _ in range(TILES)]
    for t in range(TILES):
        first, end = (0, t + 1) if above else (t, TILES)
        rows = q2[first * GROUPS * TILE : end * GROUPS * TILE]
        s = dot_nt(rows, k_aug[t * TILE : (t + 1) * TILE])
        for i in range(first, end):
            part = tile_rows(s, i - first)
            if i == t:
                part = jnp.where(mask, part, HIDDEN)
            seen[i].append(part)
    return seen


def triangle_values(probs, v_aug, above):
    total = [None] * TILES
    for t in range(TILES):
        first, end = (0, t + 1) if above else (t, TILES)
        rows = jnp.concatenate(
            [probs[i][t - i if above else t] for i in range(first, end)], axis=0
        )
        o = dot_nn(rows, v_aug[t * TILE : (t + 1) * TILE])
        for i in range(first, end):
            part = tile_rows(o, i - first)
            total[i] = part if total[i] is None else total[i] + part
    return total


def row_max(parts):
    top = parts[0]
    for part in parts[1:]:
        top = jnp.maximum(top, part)
    return jnp.max(top, axis=-1, keepdims=True)


def weights(parts, m):
    wide = jnp.concatenate([m] * (TILE // HEAD_DIM), axis=1)
    return [jnp.exp2((part - wide) * EXP_SCALE).astype(jnp.bfloat16) for part in parts]


def state_slices(base, g):
    for i in range(TILES):
        for j in range(GROUPS):
            rows = slice(base + i * TILE, base + (i + 1) * TILE)
            yield i, slice(j * TILE, (j + 1) * TILE), rows, head_cols(GROUPS * g + j)


def load_state(ref, base, g):
    parts = [[] for _ in range(TILES)]
    for i, _, rows, cols in state_slices(base, g):
        parts[i].append(ref[rows, cols])
    return [jnp.concatenate(p, axis=0) for p in parts]


def own_kernel(h, q, k, v, hot, acc, mx, ls):
    for role in range(2):
        base = role * HALF
        seen = slice(base, base + HALF)
        for g in range(PAIR):
            own = head_cols(PAIR * h + g)
            q2 = stacked_queries(q, hot, base, (PAIR * h + g) * GROUPS)
            k_aug = jnp.concatenate([k[seen, own], hot[seen, :]], axis=1)
            scores = triangle_scores(q2, k_aug, False)
            tops = [
                jnp.broadcast_to(row_max(parts), (GROUPS * TILE, HEAD_DIM)) for parts in scores
            ]
            probs = [weights(parts, m) for parts, m in zip(scores, tops)]
            o = triangle_values(probs, with_ones(v[seen, own]), False)
            for i, mine, rows, cols in state_slices(base, g):
                acc[rows, cols] = o[i][mine, :HEAD_DIM]
                ls[rows, cols] = o[i][mine, HEAD_DIM:]
                mx[rows, cols] = tops[i][mine]


STATE = jax.ShapeDtypeStruct((2 * HALF, 2 * PAIR * HEAD_DIM), jnp.float32)


def cost(gflop):
    return pl.CostEstimate(
        flops=gflop << 30, bytes_accessed=8 << 20, transcendentals=2 << 20
    )


def own(h, q, k, v, hot):
    return pl.pallas_call(
        functools.partial(own_kernel, h),
        out_shape=(STATE,) * 3,
        in_specs=[VMEM] * 4,
        out_specs=[VMEM] * 3,
        compiler_params=PARAMS,
        cost_estimate=cost(5),
    )(q, k, v, hot)


def by_head(first, second):
    return [
        x.at[:, pl.ds(part * HEAD_DIM, HEAD_DIM)] for part in range(2) for x in (first, second)
    ]


def far_kernel(h, n, idx, q, hot, zp, za, zb, pa, pb2, pb3, *rest):
    (acc0, mx0, ls0), (acc, mx, ls) = rest[:3], rest[3:6]
    far, seg, sem, seg_sem = rest[6:]
    from_partner = idx[0] >= n - 2
    id_rows = pl.ds(HALF, 8)

    def fetch(role, src):
        return pltpu.make_async_copy(src, far.at[role], sem.at[role])

    def fetch_ids(role, src):
        return pltpu.make_async_copy(src, seg.at[role], seg_sem.at[role])

    pair = pl.ds(h * SECOND, HALF)
    whole = pl.ds(0, HALF)
    back = (za.at[whole], zb)[h]
    fetch_ids(0, zp.at[id_rows]).start()
    fetch(0, zp.at[pair]).start()

    @pl.when(from_partner)
    def _():
        fetch_ids(1, pa.at[id_rows]).start()
        if h == 0:
            fetch(1, pa.at[whole]).start()
        else:
            for j, src in enumerate(by_head(pb2, pb3)):
                to = far.at[1, :, pl.ds(j * HEAD_DIM, HEAD_DIM)]
                pltpu.make_async_copy(src, to, sem.at[1]).start()

    @pl.when(jnp.logical_not(from_partner))
    def _():
        fetch_ids(1, za.at[id_rows]).start()
        fetch(1, back).start()

    for role in range(2):
        fetch_ids(role, zp.at[id_rows]).wait()
    hots = [one_hot_keys(seg[role, 0:1, :]) for role in range(2)]
    for role in range(2):
        fetch(role, zp.at[pair]).wait()

    def go(roles):
        for role in roles:
            base = role * HALF
            for g in range(PAIR):
                q2 = stacked_queries(q, hot, base, (PAIR * h + g) * GROUPS)
                keys = far[role, :, head_cols(g)]
                k_aug = jnp.concatenate([keys, hots[role]], axis=1)
                scores = triangle_scores(q2, k_aug, True)
                old = load_state(mx0, base, g)
                tops = [jnp.maximum(m, row_max(parts)) for m, parts in zip(old, scores)]
                probs = [weights(parts, m) for parts, m in zip(scores, tops)]
                v_aug = with_ones(far[role, :, head_cols(PAIR + g)])
                o = triangle_values(probs, v_aug, True)
                for i, mine, rows, cols in state_slices(base, g):
                    keep = jnp.exp2((old[i][mine] - tops[i][mine]) * EXP_SCALE)
                    acc[rows, cols] = keep * acc0[rows, cols] + o[i][mine, :HEAD_DIM]
                    ls[rows, cols] = keep * ls0[rows, cols] + o[i][mine, HEAD_DIM:]
                    mx[rows, cols] = tops[i][mine]

    @pl.when(idx[0] > 0)
    def _():
        go((0, 1))

    @pl.when(idx[0] == 0)
    def _():
        go((1,))
        for old, new in ((acc0, acc), (mx0, mx), (ls0, ls)):
            new[0:HALF, :] = old[0:HALF, :]


def far(h, n, idx, q, hot, zp, za, zb, pa, pb2, pb3, state):
    return pl.pallas_call(
        functools.partial(far_kernel, h, n),
        out_shape=(STATE,) * 3,
        in_specs=[SMEM] + [VMEM] * 2 + [ANY] * 6 + [VMEM] * 3,
        out_specs=[VMEM] * 3,
        scratch_shapes=[
            pltpu.VMEM((2, HALF, HALF), jnp.bfloat16),
            pltpu.VMEM((2, 8, HALF), jnp.bfloat16),
            pltpu.SemaphoreType.DMA((2,)),
            pltpu.SemaphoreType.DMA((2,)),
        ],
        compiler_params=PARAMS,
        cost_estimate=cost(5),
    )(idx, q, hot, zp, za, zb, pa, pb2, pb3, *state)


BOTH = ((0, 0, PAIR), (1, 1, PAIR + 1))


def finish(h, role, q, hot, piece, hot_mid, state, out, o_buf, out_sem, heads=BOTH):
    acc, mx, ls = state
    base = role * HALF
    sends = []
    for g, k_at, v_at in heads:
        q2 = stacked_queries(q, hot, base, (PAIR * h + g) * GROUPS)
        k_aug = jnp.concatenate([piece[0:HALF, head_cols(k_at)], hot_mid], axis=1)
        v_aug = with_ones(piece[0:HALF, head_cols(v_at)])
        for t in range(TILES):
            s = dot_nt(tile_rows(q2, t), k_aug)
            old = load_state(mx, base, g)[t]
            m = jnp.maximum(old, jnp.max(s, axis=-1, keepdims=True))
            keep = jnp.exp2((old - m) * EXP_SCALE)
            wide = jnp.concatenate([m] * (HALF // HEAD_DIM), axis=1)
            p = jnp.exp2((s - wide) * EXP_SCALE).astype(jnp.bfloat16)
            o = dot_nn(p, v_aug)
            for i, mine, rows, cols in state_slices(base, g):
                if i != t:
                    continue
                total = keep[mine] * ls[rows, cols] + o[mine, HEAD_DIM:]
                value = keep[mine] * acc[rows, cols] + o[mine, :HEAD_DIM]
                o_buf[rows, cols] = (value * (1.0 / total)).astype(jnp.bfloat16)
        part = pl.ds(g * GROUPS * HEAD_DIM, GROUPS * HEAD_DIM)
        to = pl.ds((PAIR * h + g) * GROUPS * HEAD_DIM, GROUPS * HEAD_DIM)
        here = pl.ds(base, HALF)
        sends.append(
            pltpu.make_async_copy(
                o_buf.at[here, part], out.at[here, to], out_sem.at[PAIR * role + g]
            )
        )
        sends[-1].start()
    return sends


def first_pair_kernel(
    n, idx, q, hot, r1, pa, pb2, pb3, d1, f1, k, v, *rest
):
    state1, state2 = rest[:3], rest[3:6]
    out, hots, mid, seg, sem, extra, extra_sem, o_buf, out_sem = rest[6:]
    odd = idx[0] % 2 == 1
    end = idx[0] == n - 1
    width = PAIR * HEAD_DIM
    whole, id_rows = pl.ds(0, HALF), pl.ds(HALF, 8)
    cols = [pl.ds(part * width, width) for part in range(2)]

    def fetch(role, ids, srcs):
        pltpu.make_async_copy(ids.at[id_rows], seg.at[role], sem.at[role, 2]).start()
        for i, src in enumerate(srcs):
            pltpu.make_async_copy(src, mid.at[role, :, cols[i]], sem.at[role, i]).start()

    def columns(ref):
        return [ref.at[whole, c] for c in cols]

    def own_front(h):
        return [x.at[whole, pl.ds(h * width, width)] for x in (k, v)]

    def fetch_extra(role, srcs):
        return [
            pltpu.make_async_copy(
                src,
                extra.at[role, :, pl.ds(i * HEAD_DIM, HEAD_DIM)],
                extra_sem.at[role, i],
            )
            for i, src in enumerate(srcs)
        ]

    for role, local, here, sent in ((0, odd, pa, r1), (1, end, None, d1)):

        @pl.when(local)
        def _():
            if role == 0:
                fetch(role, here, columns(here))
                srcs = by_head(pb2, pb3)
            else:
                fetch(role, f1, own_front(0))
                srcs = [
                    x.at[whole, pl.ds(head * HEAD_DIM, HEAD_DIM)]
                    for x in (k, v)
                    for head in (PAIR, PAIR + 1)
                ]
            for copy in fetch_extra(role, srcs):
                copy.start()

        @pl.when(jnp.logical_not(local))
        def _():
            fetch(role, sent, columns(sent))

    for role in range(2):
        for i in range(2):
            pltpu.make_async_copy(
                pa.at[whole, cols[i]], mid.at[role, :, cols[i]], sem.at[role, i]
            ).wait()
        pltpu.make_async_copy(pa.at[id_rows], seg.at[role], sem.at[role, 2]).wait()
    sends = []
    for role in range(2):
        hot_mid = one_hot_keys(seg[role, 0:1, :])
        hots[role] = hot_mid
        sends += finish(
            0, role, q, hot, mid.at[role], hot_mid, state1, out, o_buf, out_sem
        )
    for copy in sends:
        copy.wait()

    @pl.when(idx[0] == 0)
    def _():
        acc, _, ls = state2
        o_buf[0:HALF, :] = (acc[0:HALF, :] * (1.0 / ls[0:HALF, :])).astype(jnp.bfloat16)
        second = pl.ds(2 * width, 2 * width)
        copy = pltpu.make_async_copy(
            o_buf.at[whole], out.at[whole, second], out_sem.at[0]
        )
        copy.start()
        copy.wait()

    for role, local in ((0, odd), (1, end)):

        @pl.when(local)
        def _():
            for copy in fetch_extra(role, by_head(pb2, pb3)):
                copy.wait()
            for copy in finish(
                1, role, q, hot, extra.at[role], hots[role], state2, out, o_buf, out_sem
            ):
                copy.wait()


OUT_SCRATCH = (
    pltpu.VMEM((2 * HALF, 2 * PAIR * HEAD_DIM), jnp.bfloat16),
    pltpu.SemaphoreType.DMA((2 * PAIR,)),
)


def first_pair(n, idx, q, hot, pieces, state1, state2):
    piece = pltpu.VMEM((2, HALF, HALF), jnp.bfloat16)
    return pl.pallas_call(
        functools.partial(first_pair_kernel, n),
        out_shape=(
            jax.ShapeDtypeStruct(q.shape, q.dtype),
            jax.ShapeDtypeStruct((2, HALF, HEAD_DIM), jnp.bfloat16),
        ),
        in_specs=[SMEM] + [VMEM] * 2 + [ANY] * len(pieces) + [VMEM] * 6,
        out_specs=(ANY, VMEM),
        scratch_shapes=[
            piece,
            pltpu.VMEM((2, 8, HALF), jnp.bfloat16),
            pltpu.SemaphoreType.DMA((2, 3)),
            piece,
            pltpu.SemaphoreType.DMA((2, 4)),
            *OUT_SCRATCH,
        ],
        compiler_params=PARAMS,
        cost_estimate=cost(5),
        name="last0",
    )(idx, q, hot, *pieces, *state1, *state2)


ALONE = (((0, 0, 1),), ((1, 0, 1),))


def second_pair_kernel(n, idx, q, hot, *rest):
    *pieces, hots, acc, mx, ls, _, out, o_buf, out_sem = rest
    relayed = (idx[0] % 2 == 0) & (idx[0] > 0)

    def go(jobs):
        copies = []
        for role, piece, heads in jobs:
            copies += finish(
                1, role, q, hot, piece, hots[role], (acc, mx, ls), out, o_buf, out_sem, heads
            )
        for copy in copies:
            copy.wait()

    if len(pieces) == 1:

        @pl.when(relayed)
        def _():
            go([(0, pieces[0], ALONE[1])])

    else:
        front, back = pieces

        @pl.when(relayed)
        def _():
            go([(1, back, BOTH), (0, front, ALONE[0])])

        @pl.when(jnp.logical_not(relayed) & (idx[0] < n - 1))
        def _():
            go([(1, back, BOTH)])


def second_pair(n, idx, q, hot, pieces, hots, state, out):
    count = len(pieces)
    return pl.pallas_call(
        functools.partial(second_pair_kernel, n),
        out_shape=jax.ShapeDtypeStruct(q.shape, q.dtype),
        in_specs=[SMEM] + [VMEM] * (count + 6) + [ANY],
        out_specs=ANY,
        input_output_aliases={count + 7: 0},
        scratch_shapes=OUT_SCRATCH,
        compiler_params=PARAMS,
        cost_estimate=cost(5),
    )(idx, q, hot, *pieces, hots, *state, out)


def body(queries, key_states, value_states, segment_ids):
    n = lax.axis_size("seq")
    seq = lax.axis_index("seq").astype(jnp.int32)
    idx = seq.reshape(1)
    lane = jnp.arange(HEAD_DIM, dtype=jnp.int32)
    hot = (segment_ids[:, None] + 1 == lane[None, :]).astype(jnp.bfloat16)

    partner = [(i, i ^ 1) for i in range(n)]
    up_two = [(i, i + 2) for i in range(n - 2)]
    down_two = [(i + 2, i) for i in range(n - 2)]
    relay = [(i, i + 2) for i in range(0, n - 2, 2)]

    def send(x, route):
        return lax.ppermute(x, "seq", route)

    q, k, v = queries, key_states, value_states
    in_hbm = tuple(
        pltpu.with_memory_space_constraint(x, pltpu.HBM)
        for x in (k, v, segment_ids.reshape(1, 2 * HALF))
    )
    f1, front = pack_front(*in_hbm)
    pa = send(f1, partner)
    zp = send(front, up_two)
    b1, f2, f3, b2 = pack_rest(*in_hbm)
    za = send(b1, down_two)
    pb2 = send(f2, partner)
    pb3 = send(f3, partner)
    zb = send(b2, down_two)
    state1 = own(0, q, k, v, hot)
    r1 = send(pa, relay)
    state2 = own(1, q, k, v, hot)
    even = seq % 2 == 0
    back = jnp.where(even, za, b1)
    d1 = send(back, partner)
    r2 = send(pb2, relay)
    state1 = far(0, n, idx, q, hot, zp, za, za, pa, pa, pa, state1)
    back = jnp.where(even, zb, b2)
    d2 = send(back, partner)
    state2 = far(1, n, idx, q, hot, zp, za, zb, pa, pb2, pb3, state2)

    r3 = send(pb3, relay)
    pieces = (r1, pa, pb2, pb3, d1, f1, k, v)
    out, hots = first_pair(n, idx, q, hot, pieces, state1, state2)
    out = second_pair(n, idx, q, hot, (r2, d2), hots, state2, out)
    return second_pair(n, idx, q, hot, (r3,), hots, state2, out)


def solution(mesh):
    in_specs = (
        P(("grp", "seq"), "head"),
        P(("grp", "seq"), "head"),
        P(("grp", "seq"), "head"),
        P(("grp", "seq")),
    )
    out_specs = P(("grp", "seq"), "head")
    return jax.shard_map(body, mesh=mesh, in_specs=in_specs, out_specs=out_specs, check_vma=False)
```
